32 devices in a mesh: blk: 16 (over z, y, core), map: 2 (over x).
Axes of the slice: x: 2, y: 2, z: 4, core: 2. Of those that a mesh axis runs over, the one named last changes fastest.
Arguments:
- phase_history: bfloat16 [16, 2, 128, 1024], P('blk', 'map'), may hold values from -6 to 6
- tile_curvature: float32 [16], P('blk'), may hold values from 20 to 80
- interp_weights: bfloat16 [16, 512, 512], P('blk'), may hold values from -0.25 to 0.25
- strip_tiles: int32 [16, 2, 256, 1], P('blk', 'map'), may hold values from 0 to 15; in each aligned block of 256 rows (0 to 255, 256 to 511, ..., all dimensions but the last counted through in order) at most 32 rows name the same one
- row_offsets: int32 [16, 2, 256], P('blk', 'map'), may hold values from 0 to 255
- tile_owner: int32 [16], replicated, may hold values from 0 to 15, each once
Outputs:
- map_power: float32 [16, 2, 256, 512], P('blk', 'map')
The draws below stay inside these ranges and needn't reach their ends.
Inputs may be any that keep to these rules, and one draw needn't show every extreme that they name: `strip_tiles`: among the rows of one device no map tile is named more than 32 times, and in every draw some device names some tile exactly 32 times. `tile_owner`: every blk index holds exactly one map tile.
All inputs are finite; a program needn't handle non-finite values.
Results may differ from the reference program's by a relative error of at most 0.0055.
Values may be sent and summed in bfloat16 or wider, within the bound.
A program may use at most 64 MiB of HBM per device.

```python
import math
import jax
import jax.numpy as jnp
import numpy as np
from jax import lax

NB = 128
NF = 512
TR = 512
TC = 512
STOPS = 8
MAPH = 256
ROWS_DEV = 256
CAP = 32
N_BLK = 16
N_MAP = 2


def place_ends(result, own_key, low, largest):
    longest = result.shape.index(max(result.shape))
    spots = []
    for shift in (0, 1):
        where = [jax.random.randint(jax.random.fold_in(own_key, axis), (), 0, length) for axis, length in enumerate(result.shape)]
        where[longest] = (where[longest] + shift) % result.shape[longest]
        spots.append(tuple(where))
    return result.at[spots[0]].set(low).at[spots[1]].set(largest)


def levels(stream_key, shape, split, least, high):
    level = 1.0
    for dim, shards_of in split:
        draws = jax.random.uniform(jax.random.fold_in(jax.random.fold_in(stream_key, 6), dim), (shards_of,), jnp.float32, least / len(split), high / len(split))
        level = level * jnp.repeat(jnp.exp(draws), shape[dim] // shards_of).reshape((-1,) + (1,) * (len(shape) - 1 - dim))
    return level


def assign_block(key, own, number, rows, count, top, limit, slope):
    ranking = jax.random.permutation(key, count)
    crowded, common = load_shares(count, rows * top, limit, slope, True), load_shares(count, rows * top, limit, slope, False)
    places = jnp.arange(count)

    def named(sizes, rotation):
        used = int((sizes > 0).sum())
        fixed = max(1, used // 4)
        passed = fixed + (places - fixed + rotation * (used - fixed)) % max(1, count - fixed)
        return jnp.zeros((count,), jnp.int32).at[ranking[jnp.where(places < fixed, places, passed)]].set(jnp.asarray(sizes, jnp.int32))

    sizes = jnp.where(number % 4 == 0, named(crowded, number // 4), named(common, number - number // 4 - 1))
    mixed = jax.random.permutation(jax.random.fold_in(own, 3), count)
    donor, taker = mixed[0:count // 2 * 2:2], mixed[1:count // 2 * 2:2]
    room = jnp.minimum(sizes[donor] - 1, limit - sizes[taker]) // 2
    room = jnp.where((donor == ranking[0]) | (taker == ranking[0]) | (sizes[taker] == 0), 0, jnp.maximum(room, 0))
    passed = jax.random.randint(jax.random.fold_in(own, 4), (count // 2,), 0, 1 << 20) % (room + 1)
    sizes = sizes.at[donor].add(-passed).at[taker].add(passed)
    members = jnp.searchsorted(jnp.cumsum(sizes), jnp.arange(rows * top), side="right").astype(jnp.int32)
    grid = members.reshape(top, rows).T
    grid = grid[jax.random.permutation(jax.random.fold_in(own, 1), rows)]
    rotation = jax.random.randint(jax.random.fold_in(own, 2), (rows, 1), 0, top)
    return jnp.take_along_axis(grid, (jnp.arange(top)[None, :] + rotation) % top, axis=1)


def load_shares(count, total, most, skew, full):
    weights = [(1 << 20) // math.isqrt(rank ** skew) + 1 for rank in range(1, count + 1)]
    largest = most if full else min(most, max(-(-total // count), total * weights[0] // sum(weights)))
    least = 1 if total - largest >= count - 1 else 0
    given, surplus = [largest] + [least] * (count - 1), total - largest - least * (count - 1)
    while surplus > 0:
        free = [i for i in range(1, count) if given[i] < largest] or [i for i in range(1, count) if given[i] < most]
        mass, left = sum([weights[i] for i in free]), surplus
        for i in free:
            addition = min(most - given[i], max(1, left * weights[i] // mass), surplus)
            given[i] = given[i] + addition
            surplus = surplus - addition
    return np.array(given)


def normal_values(own_key, shape, width, most, cuts=(), kind=jnp.bfloat16):
    drawn = width * jax.random.normal(own_key, shape, jnp.float32)
    if cuts:
        drawn = drawn * levels(own_key, shape, cuts, -0.22, 0.18)
    return jnp.clip(drawn, -most, most).astype(kind)


def setup_inputs(seed: int = 0) -> dict:
    key_of = jax.random.split(jax.random.key(seed), 7)
    phase_history = normal_values(key_of[0], (N_BLK, N_MAP, NB, 2 * NF), 1.0, 6.0, ((0, 16), (1, 2)))
    tile_curvature = jnp.clip(20.0 + 60.0 * jax.random.uniform(key_of[1], (N_BLK,), jnp.float32) ** levels(key_of[1], (N_BLK,), ((0, 16),), -0.2, 0.2), 20.0, 80.0)
    interp_weights = normal_values(key_of[2], (N_BLK, TC, TC), TC ** -0.5, 0.25, ((0, 16),))
    strip_tiles_keys = jax.random.split(jax.random.fold_in(key_of[3], 1), N_BLK * N_MAP * ROWS_DEV // ROWS_DEV)
    strip_tiles_turns = jax.random.permutation(jax.random.fold_in(key_of[3], 3), N_BLK * N_MAP * ROWS_DEV // ROWS_DEV)
    strip_tiles = jax.vmap(lambda own, number: assign_block(jax.random.fold_in(key_of[3], 2), own, number, ROWS_DEV, N_BLK, 1, CAP, 2))(strip_tiles_keys, strip_tiles_turns).reshape((N_BLK, N_MAP, ROWS_DEV, 1))
    row_offsets = place_ends(jax.random.randint(key_of[4], (N_BLK, N_MAP, ROWS_DEV), 0, MAPH), jax.random.fold_in(key_of[4], 1), 0, MAPH - 1).astype(jnp.int32)
    tile_owner = jax.random.permutation(key_of[5], N_BLK).astype(jnp.int32)
    return {"phase_history": phase_history, "tile_curvature": tile_curvature, "interp_weights": interp_weights, "strip_tiles": strip_tiles, "row_offsets": row_offsets, "tile_owner": tile_owner}


def range_matrix(freq_count, column_count):
    freq_index = jnp.arange(freq_count, dtype=jnp.int32)[:, None]
    column_index = jnp.arange(column_count, dtype=jnp.int32)[None, :]
    angle = (freq_index * column_index % freq_count).astype(jnp.float32) * (2.0 * math.pi / freq_count)
    factor = 1.0 / math.sqrt(freq_count)
    real_part = jnp.cos(angle) * factor
    imag_part = -jnp.sin(angle) * factor
    upper = jnp.concatenate([real_part, imag_part], axis=1)
    lower = jnp.concatenate([-imag_part, real_part], axis=1)
    return jnp.concatenate([upper, lower], axis=0).astype(jnp.bfloat16)

def cross_rows(stop_index, map_index, row_index, map_count, pulse_count, span):
    pulse_index = jnp.arange(pulse_count, dtype=jnp.int32)[None, :]
    along = (stop_index * map_count + map_index) * pulse_count + pulse_index
    angle = (row_index[:, None] * along % span).astype(jnp.float32) * (2.0 * math.pi / span)
    factor = 1.0 / math.sqrt(span)
    return jnp.concatenate([jnp.cos(angle) * factor, -jnp.sin(angle) * factor], axis=1).astype(jnp.bfloat16)

def apply_phase(source_block, curvature, stop_index, map_index, map_count, pulse_count, freq_count, span):
    pulse_index = jnp.arange(pulse_count, dtype=jnp.int32)
    along = ((stop_index * map_count + map_index) * pulse_count + pulse_index).astype(jnp.float32) / span - 0.5
    relative = jnp.arange(freq_count, dtype=jnp.int32).astype(jnp.float32) / freq_count - 0.5
    phase_angle = curvature * (along * along)[:, None] * (1.0 + relative[None, :])
    cosine = jnp.cos(phase_angle)
    sine = jnp.sin(phase_angle)
    values = source_block.astype(jnp.float32)
    real_part = values[:, :freq_count]
    imag_part = values[:, freq_count:]
    return jnp.concatenate([real_part * cosine - imag_part * sine, real_part * sine + imag_part * cosine], axis=1).astype(jnp.bfloat16)

def stack_spectrum(spectrum_now):
    half_width = spectrum_now.shape[1] // 2
    real_part = spectrum_now[:, :half_width]
    imag_part = spectrum_now[:, half_width:]
    upper = jnp.concatenate([real_part, imag_part], axis=1)
    lower = jnp.concatenate([-imag_part, real_part], axis=1)
    return jnp.concatenate([upper, lower], axis=0)

def tile_image(tile_index, phase_history, curvature):
    lead_count = STOPS // 2 - 1
    span = STOPS * N_MAP * NB
    ranges = range_matrix(NF, TC).astype(jnp.float32)
    row_index = jnp.arange(TR, dtype=jnp.int32)
    running = jnp.zeros((TR, 2 * TC), jnp.float32)
    for stop_index in range(STOPS):
        source = ((tile_index + stop_index - lead_count) % N_BLK).astype(jnp.int32)
        column_blocks = lax.dynamic_index_in_dim(phase_history, source, 0, keepdims=False)
        for map_index in range(N_MAP):
            phased = apply_phase(column_blocks[map_index], curvature, stop_index, map_index, N_MAP, NB, NF, span)
            spectrum_now = jnp.dot(phased.astype(jnp.float32), ranges, precision=lax.Precision.HIGHEST).astype(jnp.bfloat16)
            crossing = cross_rows(stop_index, map_index, row_index, N_MAP, NB, span).astype(jnp.float32)
            running = running + jnp.dot(crossing, stack_spectrum(spectrum_now).astype(jnp.float32), precision=lax.Precision.HIGHEST)
    return running.astype(jnp.bfloat16)

def reference(phase_history, tile_curvature, interp_weights, strip_tiles, row_offsets, tile_owner):

    def one_tile(tile_index):
        return tile_image(tile_index, phase_history, tile_curvature[tile_index])
    images = lax.map(one_tile, jnp.arange(N_BLK, dtype=jnp.int32))
    strip_rows = images.reshape(N_BLK, N_MAP, ROWS_DEV, 2 * TC)
    destination = tile_owner[strip_tiles[..., 0]].astype(jnp.int32)
    slot_count = N_BLK * CAP
    results = []
    for map_index in range(N_MAP):
        flat_rows = strip_rows[:, map_index].reshape(N_BLK * ROWS_DEV, 2 * TC)
        flat_dest = destination[:, map_index].reshape(N_BLK * ROWS_DEV)
        flat_offsets = row_offsets[:, map_index].reshape(N_BLK * ROWS_DEV).astype(jnp.int32)
        sorted_rows = jnp.argsort(flat_dest, stable=True).astype(jnp.int32)
        holder_counts = lax.optimization_barrier(jnp.sum((flat_dest[:, None] == jnp.arange(N_BLK, dtype=jnp.int32)[None, :]).astype(jnp.int32), axis=0)).astype(jnp.int32)
        holder_starts = (jnp.cumsum(holder_counts) - holder_counts).astype(jnp.int32)
        padded_rows = jnp.concatenate([sorted_rows, jnp.zeros((slot_count,), jnp.int32)])

        def one_holder(holder):
            picked = lax.dynamic_slice_in_dim(padded_rows, holder_starts[holder], slot_count)
            usable = jnp.arange(slot_count, dtype=jnp.int32) < holder_counts[holder]
            chosen = flat_rows[picked].astype(jnp.float32)
            weights = interp_weights[holder].astype(jnp.float32)
            real_out = jnp.dot(chosen[:, :TC], weights, precision=lax.Precision.HIGHEST)
            imag_out = jnp.dot(chosen[:, TC:], weights, precision=lax.Precision.HIGHEST)
            power_rows = real_out * real_out + imag_out * imag_out
            target = jnp.where(usable, flat_offsets[picked], MAPH).astype(jnp.int32)
            return jnp.zeros((MAPH, TC), jnp.float32).at[target].add(power_rows, mode='drop')
        results.append(lax.map(one_holder, jnp.arange(N_BLK, dtype=jnp.int32)))
    return jnp.stack(results, axis=1)
```

```python
import functools
import math

import jax
import jax.numpy as jnp
import numpy as np
from jax import lax
from jax.experimental import pallas as pl
from jax.experimental.pallas import tpu as pltpu
from jax.sharding import PartitionSpec as P

STOPS = 8
MAPH = 256
LANES = 128
TILE = 16


def fit_turns():
    z = 0.125 - 0.125 * np.cos(np.pi * (np.arange(400) + 0.5) / 400)
    t = np.sqrt(z)
    cheb = np.polynomial.chebyshev.Chebyshev
    cos_fit = cheb.fit(z, np.cos(2 * np.pi * t), 7, domain=[0, 0.25])
    sin_fit = cheb.fit(z, np.sin(2 * np.pi * t) / t, 6, domain=[0, 0.25])
    power = np.polynomial.Polynomial
    return (
        [float(np.float32(c)) for c in cos_fit.convert(kind=power).coef],
        [float(np.float32(c)) for c in sin_fit.convert(kind=power).coef],
    )


COS_COEF, SIN_COEF = fit_turns()


def cos_sin_turns(turns):
    t = turns - jnp.round(turns)
    z = t * t
    c = jnp.full_like(z, COS_COEF[-1])
    for coef in COS_COEF[-2::-1]:
        c = c * z + coef
    s = jnp.full_like(z, SIN_COEF[-1])
    for coef in SIN_COEF[-2::-1]:
        s = s * z + coef
    return c, s * t


def iota(shape, axis):
    return lax.broadcasted_iota(jnp.int32, shape, axis)


def kernel(
    sizes,
    block_hbm, curv_ref, weight_hbm, tiles_hbm, offs_hbm, owner_hbm,
    out_ref,
    weight_ref, tiles_ref, offs_ref, owner_ref, in_sem, trig, blocks, ranges, cross, phased, right, weights, x_send, x_recv, x_own, packed, arrived, slot_hot,
    o_send, o_recv, u_acc, v_acc,
    g_send, g_recv, xs_sem, xr_sem, as_sem, ar_sem, os_sem, or_sem,
):
    blk, maps, pulses, freqs, columns, rows, cap = sizes
    f32, bf16 = jnp.float32, jnp.bfloat16
    me = lax.axis_index("blk")
    my_map = lax.axis_index("map")
    other_map = 1 - my_map
    core = lax.rem(me, 2)
    span = STOPS * maps * pulses
    stacked = STOPS // 2 * pulses
    chunks = columns // LANES
    width = 2 * LANES
    slots = blk * cap
    own_stop = STOPS // 2 - 1

    def device(index):
        return (lax.rem(index + 2 * blk, blk), my_map)

    mesh_id = pl.DeviceIdType.MESH

    barrier = pltpu.get_barrier_semaphore()

    def greet(i, _):
        pl.semaphore_signal(barrier, inc=1, device_id=device(me + i), device_id_type=mesh_id)
        return 0

    lax.fori_loop(1, blk, greet, 0)
    pl.semaphore_signal(barrier, inc=1, device_id=(me, other_map), device_id_type=mesh_id)

    def bring(source, target, sem):
        return pltpu.make_async_copy(source, target, in_sem.at[sem])

    inputs = [
        bring(block_hbm, blocks.at[own_stop], 0),
        bring(owner_hbm, owner_ref, 1),
        bring(tiles_hbm, tiles_ref, 2),
        bring(offs_hbm, offs_ref, 3),
        bring(weight_hbm, weight_ref, 4),
    ]
    for copy in inputs:
        copy.start()
    inputs[0].wait()
    block_ref = blocks.at[own_stop]
    pl.semaphore_wait(barrier, blk)

    def push(source, stop, target, sem):
        return pltpu.make_async_remote_copy(
            src_ref=source, dst_ref=blocks.at[stop], send_sem=g_send.at[sem],
            recv_sem=g_recv.at[stop], device_id=target, device_id_type=mesh_id)

    def arrived_block(stop):
        pltpu.make_async_copy(blocks.at[stop], blocks.at[stop], g_recv.at[stop]).wait()

    partner = device(me + 1 - 2 * core)
    shift = 2 * core - 1

    push(block_ref, 7, device(me - 4), 0).start()

    @pl.when(core == 1)
    def _():
        push(block_ref, 0, device(me + 3), 6).start()

    push(block_ref, 5, device(me - 2), 1).start()
    push(block_ref, 1, device(me + 2), 2).start()
    push(block_ref, own_stop + shift, partner, 3).start()

    half_freqs = freqs // 2
    half_chunks = chunks // 2
    half_rows = rows // 2

    def fill_ranges(i, _):
        at = pl.ds(pl.multiple_of(i * TILE, TILE), TILE)
        below = pl.ds(pl.multiple_of(half_freqs + i * TILE, TILE), TILE)
        f = (i * TILE + iota((TILE, columns // 2), 0)).astype(f32)
        for odd in range(2):
            c = (2 * iota((TILE, columns // 2), 1) + odd).astype(f32)
            re, im = cos_sin_turns(f * c * (1.0 / freqs))
            re = (re * (1.0 / math.sqrt(freqs))).astype(bf16)
            im = (im * (1.0 / math.sqrt(freqs)))
            pos, neg = im.astype(bf16), (-im).astype(bf16)
            for n in range(half_chunks):
                cut = slice(n * LANES, (n + 1) * LANES)
                to = odd * half_chunks + n
                ranges[to, at, 0:LANES] = re[:, cut]
                ranges[to, at, LANES:width] = neg[:, cut]
                ranges[to, below, 0:LANES] = pos[:, cut]
                ranges[to, below, LANES:width] = re[:, cut]
        return 0

    lax.fori_loop(0, half_freqs // TILE, fill_ranges, 0)

    lane = iota((1, stacked), 1)
    q_lane = (lane + (lax.div(lane, pulses) * (maps - 1) + my_map) * pulses).astype(f32)

    def fill_cross(i, _):
        at = pl.ds(pl.multiple_of(i * TILE, TILE), TILE)
        g = i * TILE
        odd = lax.div(g, rows)
        own = lax.div(lax.rem(g, rows), half_rows)
        part = jnp.where(own == 1, my_map, other_map)
        base = part * rows + odd + 2 * lax.rem(g, half_rows)
        a = (base + 2 * iota((TILE, stacked), 0)).astype(f32)
        re, im = cos_sin_turns(a * q_lane * (1.0 / span))
        cross[at, 0:stacked] = (re * (1.0 / math.sqrt(span))).astype(bf16)
        cross[at, stacked:2 * stacked] = (im * (-1.0 / math.sqrt(span))).astype(bf16)
        return 0

    lax.fori_loop(0, rows * maps // TILE, fill_cross, 0)

    def fill_slots():
        tiles = tiles_ref[...]
        holders = iota((blk, rows), 0)
        named = (holders == tiles).astype(f32).astype(bf16)
        holds = (iota((blk, blk), 0) == owner_ref[...]).astype(f32).astype(bf16)
        hot = jnp.dot(holds, named, preferred_element_type=f32)
        dest = jnp.sum(holders.astype(f32) * hot, axis=0, keepdims=True).astype(jnp.int32)
        upto = (iota((rows, rows), 0) <= iota((rows, rows), 1)).astype(f32).astype(bf16)
        counts = jnp.dot(hot.astype(bf16), upto, preferred_element_type=f32)
        rank = jnp.sum(counts * hot, axis=0, keepdims=True).astype(jnp.int32) - 1
        slot = dest * cap + rank
        spot = iota((rows, rows), 1)
        spot = 2 * lax.rem(spot, half_rows) + lax.div(spot, half_rows)
        order = (iota((rows, rows), 0) == spot).astype(f32).astype(bf16)
        for i in range(slots // LANES):
            at = i * LANES + iota((LANES, rows), 0)
            hits = (at == slot).astype(f32).astype(bf16)
            slot_hot[i * LANES:(i + 1) * LANES, :] = jnp.dot(
                hits, order, preferred_element_type=f32).astype(bf16)
        place = lax.rem(me, LANES // cap) * cap + rank
        marks = jnp.where(iota((LANES, rows), 0) == place, (offs_ref[...] + 1).astype(f32), 0.0)
        table = lax.dot_general(
            hot.astype(bf16), marks.astype(bf16), (((1,), (1,)), ((), ())),
            preferred_element_type=f32)
        for d in range(blk):
            o_send[d] = table[d:d + 1, :]
        o_recv[me] = o_send[me]

        def send(i, _):
            to = lax.rem(me + i, blk)
            pltpu.make_async_remote_copy(
                src_ref=o_send.at[to], dst_ref=o_recv.at[me], send_sem=os_sem,
                recv_sem=or_sem, device_id=(to, my_map), device_id_type=mesh_id).start()
            return 0

        lax.fori_loop(1, blk, send, 0)

    for copy in inputs[1:]:
        copy.wait()
    fill_slots()

    def order_weights(i, _):
        at = pl.ds(pl.multiple_of(i * LANES, LANES), LANES)
        r = i * LANES + iota((LANES, columns), 0)
        r = 2 * lax.rem(r, columns // 2) + lax.div(r, columns // 2)
        order = (iota((LANES, columns), 1) == r).astype(f32).astype(bf16)
        weights[at, :] = jnp.dot(
            order, weight_ref[...], preferred_element_type=f32).astype(bf16)
        return 0

    lax.fori_loop(0, chunks, order_weights, 0)

    def fill_trig(i, _):
        at = pl.ds(pl.multiple_of(lax.rem(i, pulses // TILE) * TILE, TILE), TILE)
        k = lax.div(i, pulses // TILE)
        q = (k * maps + my_map) * pulses + lax.rem(i, pulses // TILE) * TILE + iota((TILE, 1), 0)
        s = q.astype(f32) * (1.0 / span) - 0.5
        r = iota((TILE, freqs), 1).astype(f32) * (1.0 / freqs) - 0.5
        angle = curv_ref[0] * (s * s) * (1.0 + r)
        c, si = cos_sin_turns(angle * (0.5 / math.pi))
        trig[k, 0, at, :] = c
        trig[k, 1, at, :] = si
        return 0

    lax.fori_loop(0, STOPS * pulses // TILE, fill_trig, 0)

    def turned(k, i):
        at = pl.ds(pl.multiple_of(i * TILE, TILE), TILE)
        c, si = trig[k, 0, at, :], trig[k, 1, at, :]
        re = blocks[k, at, 0:freqs].astype(f32)
        im = blocks[k, at, freqs:2 * freqs].astype(f32)
        return re * c - im * si, re * si + im * c

    def phase(j):
        def turn(i, _):
            first = turned(j, i)
            second = turned(j + STOPS // 2, i)
            for part in range(2):
                z_sum, z_diff = first[part] + second[part], first[part] - second[part]
                to = slice(part * half_freqs, (part + 1) * half_freqs)
                for odd_row, z in ((0, z_sum), (1, z_diff)):
                    at = pl.ds(pl.multiple_of(odd_row * pulses + i * TILE, TILE), TILE)
                    near, far = z[:, :half_freqs], z[:, half_freqs:]
                    phased[0, at, to] = (near + far).astype(bf16)
                    phased[1, at, to] = (near - far).astype(bf16)
            return 0

        lax.fori_loop(0, pulses // TILE, turn, 0, unroll=2)

    def spectrum(j, n):
        top = pl.ds(pl.multiple_of(j * pulses, pulses), pulses)
        low = pl.ds(pl.multiple_of(stacked + j * pulses, pulses), pulses)
        odd = lax.div(n, half_chunks)
        y = jnp.dot(phased[odd], ranges[n], preferred_element_type=f32)
        yr, yi = y[:, :LANES], y[:, LANES:]
        for odd_row in range(2):
            cut = slice(odd_row * pulses, (odd_row + 1) * pulses)
            real, imag = yr[cut].astype(bf16), yi[cut].astype(bf16)
            right[n, odd_row, top, 0:LANES] = real
            right[n, odd_row, top, LANES:width] = imag
            right[n, odd_row, low, 0:LANES] = (-yi[cut]).astype(bf16)
            right[n, odd_row, low, LANES:width] = real

    def step(i, _):
        j = jnp.where(i == 0, 1, jnp.where(i == 1, 3, jnp.where(i == 2, 0, 2)))

        @pl.when(i == 0)
        def _():
            arrived_block(5)
            push(blocks.at[5], 5 + shift, partner, 4).start()
            arrived_block(1)
            push(blocks.at[1], 1 + shift, partner, 5).start()

        @pl.when(i == 1)
        def _():
            arrived_block(7)

            @pl.when(core == 0)
            def _():
                push(blocks.at[7], 6, partner, 6).start()

        @pl.when(i >= 2)
        def _():
            arrived_block(j)
            arrived_block(j + STOPS // 2)

        phase(j)

        @pl.when(i < STOPS // 2 - 1)
        def _():
            for n in range(chunks):
                spectrum(j, n)

        return 0

    lax.fori_loop(0, STOPS // 2, step, 0)
    last = 2

    first_parts = 2
    parts = chunks + first_parts - 1

    def part_of(s):
        if s < first_parts:
            return 0, pl.ds(s * LANES, LANES), slice(s * LANES, (s + 1) * LANES)
        return s - first_parts + 1, pl.ds(0, width), slice(0, width)

    def x_copy(s):
        n, lanes, _ = part_of(s)
        return pltpu.make_async_remote_copy(
            src_ref=x_send.at[n, :, lanes], dst_ref=x_recv.at[n, :, lanes], send_sem=xs_sem.at[s],
            recv_sem=xr_sem.at[s], device_id=(me, other_map), device_id_type=mesh_id)

    own_slots = pl.ds(pl.multiple_of(me * cap, cap), cap)

    def produce(n):
        spectrum(last, n)
        for odd_row in range(2):
            table = cross[odd_row * rows:(odd_row + 1) * rows, :]
            y = jnp.dot(table, right[n, odd_row], preferred_element_type=f32)
            to = slice(odd_row * half_rows, (odd_row + 1) * half_rows)
            x_send[n, to, :] = y[:half_rows].astype(bf16)
            x_own[n, to, :] = y[half_rows:]
        for s in range(parts):
            if part_of(s)[0] == n:
                x_copy(s).start()

    def route(s):
        n, lanes, cut = part_of(s)
        x_copy(s).wait_recv()
        image = (x_own[n, :, cut] + x_recv[n, :, cut].astype(f32)).astype(bf16)
        packed[n, :, cut] = jnp.dot(
            slot_hot[...], image, preferred_element_type=f32).astype(bf16)

        def send(i, _):
            to = lax.rem(me + i, blk)
            pltpu.make_async_remote_copy(
                src_ref=packed.at[n, pl.ds(pl.multiple_of(to * cap, cap), cap), lanes],
                dst_ref=arrived.at[n, own_slots, lanes], send_sem=as_sem.at[s],
                recv_sem=ar_sem.at[s], device_id=(to, my_map),
                device_id_type=mesh_id).start()
            return 0

        lax.fori_loop(1, blk, send, 0)
        arrived[n, own_slots, cut] = packed[n, own_slots, cut]

    produce(0)
    for s in range(parts):
        n = part_of(s)[0]
        if (s == 0 or part_of(s - 1)[0] != n) and n + 1 < chunks:
            produce(n + 1)
        route(s)

    def wait_bytes(ref, sem):
        pltpu.make_async_copy(ref, ref, sem).wait()

    others = pl.ds(0, (blk - 1) * cap)
    u_acc[...] = jnp.zeros_like(u_acc)
    v_acc[...] = jnp.zeros_like(v_acc)

    def interp(s):
        n, lanes, cut = part_of(s)
        wait_bytes(arrived.at[n, others, lanes], ar_sem.at[s])
        w = weights[n * LANES:(n + 1) * LANES, :]
        for acc, at in ((u_acc, 0), (v_acc, LANES)):
            if cut.start <= at < cut.stop:
                acc[...] += jnp.dot(
                    arrived[n, :, at:at + LANES], w, preferred_element_type=f32)

    for s in range(parts):
        interp(s)
    wait_bytes(o_recv.at[pl.ds(0, blk - 1)], or_sem)
    per = LANES // cap
    pieces = []
    for g in range(blk // per):
        total = o_recv[g * per]
        for j in range(1, per):
            total = total + o_recv[g * per + j]
        pieces.append(total)
    total = jnp.zeros((MAPH, columns), f32)
    for g in range(slots // LANES):
        cut = slice(g * LANES, (g + 1) * LANES)
        spot = iota((MAPH, LANES), 0) == pieces[g].astype(jnp.int32) - 1
        spot = spot.astype(f32).astype(bf16)
        u, v = u_acc[cut, :], v_acc[cut, :]
        power = u * u + v * v
        high = power.astype(bf16)
        rest = power - high.astype(f32)
        mid = rest.astype(bf16)
        for part in (high, mid):
            total = total + jnp.dot(spot, part, preferred_element_type=f32)
    out_ref[...] = total

    for sem in range(7):
        wait_bytes(blocks.at[0], g_send.at[sem])
    for s in range(parts):
        n, lanes, _ = part_of(s)
        wait_bytes(x_send.at[n, :, lanes], xs_sem.at[s])
        wait_bytes(packed.at[n, others, lanes], as_sem.at[s])
    wait_bytes(o_send.at[pl.ds(0, blk - 1)], os_sem)


def body(phase_history, tile_curvature, interp_weights, strip_tiles, row_offsets, tile_owner):
    blk = lax.axis_size("blk")
    maps = lax.axis_size("map")
    pulses = phase_history.shape[2]
    freqs = phase_history.shape[3] // 2
    columns = interp_weights.shape[2]
    rows = strip_tiles.shape[2]
    cap = max(TILE, 2 * rows // blk)
    slots = blk * cap
    chunks = columns // LANES
    width = 2 * LANES
    stacked = STOPS // 2 * pulses
    f32, bf16 = jnp.float32, jnp.bfloat16
    hbm = pl.BlockSpec(memory_space=pltpu.HBM)
    vmem = pl.BlockSpec(memory_space=pltpu.VMEM)
    dma = pltpu.SemaphoreType.DMA
    in_hbm = functools.partial(pltpu.with_memory_space_constraint, memory_space=pltpu.HBM)
    out = pl.pallas_call(
        functools.partial(kernel, (blk, maps, pulses, freqs, columns, rows, cap)),
        out_shape=jax.ShapeDtypeStruct((MAPH, columns), f32),
        in_specs=[hbm, pl.BlockSpec(memory_space=pltpu.SMEM), hbm, hbm, hbm, hbm],
        out_specs=vmem,
        scratch_shapes=[
            pltpu.VMEM((columns, columns), bf16),
            pltpu.VMEM((1, rows), jnp.int32),
            pltpu.VMEM((1, rows), jnp.int32),
            pltpu.VMEM((1, blk), jnp.int32),
            dma((5,)),
            pltpu.VMEM((STOPS, 2, pulses, freqs), f32),
            pltpu.VMEM((STOPS, pulses, 2 * freqs), bf16),
            pltpu.VMEM((chunks, freqs, width), bf16),
            pltpu.VMEM((rows * maps, 2 * stacked), bf16),
            pltpu.VMEM((2, 2 * pulses, freqs), bf16),
            pltpu.VMEM((chunks, 2, 2 * stacked, width), bf16),
            pltpu.VMEM((columns, columns), bf16),
            pltpu.VMEM((chunks, rows, width), bf16),
            pltpu.VMEM((chunks, rows, width), bf16),
            pltpu.VMEM((chunks, rows, width), f32),
            pltpu.VMEM((chunks, slots, width), bf16),
            pltpu.VMEM((chunks, slots, width), bf16),
            pltpu.VMEM((slots, rows), bf16),
            pltpu.VMEM((blk, 1, LANES), f32),
            pltpu.VMEM((blk, 1, LANES), f32),
            pltpu.VMEM((slots, columns), f32),
            pltpu.VMEM((slots, columns), f32),
            dma((7,)), dma((STOPS,)), dma((chunks + 1,)), dma((chunks + 1,)),
            dma((chunks + 1,)), dma((chunks + 1,)), dma, dma,
        ],
        compiler_params=pltpu.CompilerParams(
            collective_id=0, has_side_effects=True, vmem_limit_bytes=40 * 2**20),
    )(
        in_hbm(phase_history[0, 0]), tile_curvature, in_hbm(interp_weights[0]),
        in_hbm(strip_tiles[0, 0].reshape(1, rows)), in_hbm(row_offsets[0]),
        in_hbm(tile_owner.reshape(1, blk)),
    )
    return jnp.maximum(out, 0.0).reshape(1, 1, MAPH, columns)


def solution(mesh):
    in_specs = (
        P("blk", "map", None, None),
        P("blk"),
        P("blk", None, None),
        P("blk", "map", None, None),
        P("blk", "map", None),
        P(),
    )
    out_specs = P("blk", "map", None, None)
    return jax.shard_map(body, mesh=mesh, in_specs=in_specs, out_specs=out_specs, check_vma=False)
```

```python
import functools
import math

import jax
import jax.numpy as jnp
import numpy as np
from jax import lax
from jax.experimental import pallas as pl
from jax.experimental.pallas import tpu as pltpu
from jax.sharding import PartitionSpec as P

STOPS = 8
MAPH = 256
LANES = 128
TILE = 16


def fit_turns():
    z = 0.125 - 0.125 * np.cos(np.pi * (np.arange(400) + 0.5) / 400)
    t = np.sqrt(z)
    cheb = np.polynomial.chebyshev.Chebyshev
    cos_fit = cheb.fit(z, np.cos(2 * np.pi * t), 7, domain=[0, 0.25])
    sin_fit = cheb.fit(z, np.sin(2 * np.pi * t) / t, 6, domain=[0, 0.25])
    power = np.polynomial.Polynomial
    return (
        [float(np.float32(c)) for c in cos_fit.convert(kind=power).coef],
        [float(np.float32(c)) for c in sin_fit.convert(kind=power).coef],
    )


COS_COEF, SIN_COEF = fit_turns()


def cos_sin_turns(turns):
    t = turns - jnp.round(turns)
    z = t * t
    c = jnp.full_like(z, COS_COEF[-1])
    for coef in COS_COEF[-2::-1]:
        c = c * z + coef
    s = jnp.full_like(z, SIN_COEF[-1])
    for coef in SIN_COEF[-2::-1]:
        s = s * z + coef
    return c, s * t


def iota(shape, axis):
    return lax.broadcasted_iota(jnp.int32, shape, axis)


def kernel(
    sizes,
    block_hbm, curv_ref, weight_hbm, tiles_hbm, offs_hbm, owner_hbm,
    out_ref,
    weight_ref, tiles_ref, offs_ref, owner_ref, in_sem, trig, blocks, ranges, cross, phased, right, weights, x_send, x_recv, x_own, packed, arrived, slot_hot,
    o_send, o_recv, u_acc, v_acc,
    g_send, g_recv, xs_sem, xr_sem, as_sem, ar_sem, os_sem, or_sem,
):
    blk, maps, pulses, freqs, columns, rows, cap = sizes
    f32, bf16 = jnp.float32, jnp.bfloat16
    me = lax.axis_index("blk")
    my_map = lax.axis_index("map")
    other_map = 1 - my_map
    core = lax.rem(me, 2)
    span = STOPS * maps * pulses
    stacked = STOPS // 2 * pulses
    chunks = columns // LANES
    width = 2 * LANES
    slots = blk * cap
    own_stop = STOPS // 2 - 1

    def device(index):
        return (lax.rem(index + 2 * blk, blk), my_map)

    mesh_id = pl.DeviceIdType.MESH

    barrier = pltpu.get_barrier_semaphore()

    def greet(i, _):
        pl.semaphore_signal(barrier, inc=1, device_id=device(me + i), device_id_type=mesh_id)
        return 0

    lax.fori_loop(1, blk, greet, 0)
    pl.semaphore_signal(barrier, inc=1, device_id=(me, other_map), device_id_type=mesh_id)

    def bring(source, target, sem):
        return pltpu.make_async_copy(source, target, in_sem.at[sem])

    inputs = [
        bring(block_hbm, blocks.at[own_stop], 0),
        bring(owner_hbm, owner_ref, 1),
        bring(tiles_hbm, tiles_ref, 2),
        bring(offs_hbm, offs_ref, 3),
        bring(weight_hbm, weight_ref, 4),
    ]
    for copy in inputs:
        copy.start()
    inputs[0].wait()
    pl.semaphore_wait(barrier, blk)

    partner = device(me + 1 - 2 * core)
    shift = 2 * core - 1
    quad = lax.rem(me, 4)
    half = pulses // 2
    last = 2 - core

    def half_of(stop, h):
        return blocks.at[stop, pl.ds(h * half, half)]

    def push(source, stop, h, target, kind):
        pltpu.make_async_remote_copy(
            src_ref=half_of(source, h), dst_ref=half_of(stop, h), send_sem=g_send.at[kind, h],
            recv_sem=g_recv.at[stop, h], device_id=target, device_id_type=mesh_id).start()

    def push_own(stop, target, kind):
        for h in range(2):
            push(own_stop, stop, h, target, kind)

    def arrived_half(stop, h):
        pltpu.make_async_copy(half_of(stop, h), half_of(stop, h), g_recv.at[stop, h]).wait()

    def arrived_block(stop):
        for h in range(2):
            arrived_half(stop, h)

    def pass_on(stop, to_stop, target, kind):
        for h in range(2):
            arrived_half(stop, h)
            push(stop, to_stop, h, target, kind)

    @pl.when(quad == 3)
    def _():
        push_own(0, device(me + 3), 1)

    push_own(7, device(me - 4), 0)

    @pl.when(quad == 1)
    def _():
        push_own(0, device(me + 3), 1)

    @pl.when(quad != 1)
    def _():
        push_own(5, device(me - 2), 2)

    @pl.when(quad != 3)
    def _():
        push_own(1, device(me + 2), 3)

    push_own(own_stop + shift, partner, 4)

    half_freqs = freqs // 2
    half_chunks = chunks // 2
    half_rows = rows // 2

    def fill_ranges(i, _):
        at = pl.ds(pl.multiple_of(i * TILE, TILE), TILE)
        below = pl.ds(pl.multiple_of(half_freqs + i * TILE, TILE), TILE)
        f = (i * TILE + iota((TILE, columns // 2), 0)).astype(f32)
        for odd in range(2):
            c = (2 * iota((TILE, columns // 2), 1) + odd).astype(f32)
            re, im = cos_sin_turns(f * c * (1.0 / freqs))
            re = (re * (1.0 / math.sqrt(freqs))).astype(bf16)
            im = (im * (1.0 / math.sqrt(freqs)))
            pos, neg = im.astype(bf16), (-im).astype(bf16)
            for n in range(half_chunks):
                cut = slice(n * LANES, (n + 1) * LANES)
                to = odd * half_chunks + n
                ranges[to, at, 0:LANES] = re[:, cut]
                ranges[to, at, LANES:width] = neg[:, cut]
                ranges[to, below, 0:LANES] = pos[:, cut]
                ranges[to, below, LANES:width] = re[:, cut]
        return 0

    lax.fori_loop(0, half_freqs // TILE, fill_ranges, 0)

    lane = iota((1, stacked), 1)
    q_lane = (lane + (lax.div(lane, pulses) * (maps - 1) + my_map) * pulses).astype(f32)

    def fill_cross(i, _):
        at = pl.ds(pl.multiple_of(i * TILE, TILE), TILE)
        g = i * TILE
        odd = lax.div(g, rows)
        own = lax.div(lax.rem(g, rows), half_rows)
        part = jnp.where(own == 1, my_map, other_map)
        base = part * rows + odd + 2 * lax.rem(g, half_rows)
        a = (base + 2 * iota((TILE, stacked), 0)).astype(f32)
        re, im = cos_sin_turns(a * q_lane * (1.0 / span))
        cross[at, 0:stacked] = (re * (1.0 / math.sqrt(span))).astype(bf16)
        cross[at, stacked:2 * stacked] = (im * (-1.0 / math.sqrt(span))).astype(bf16)
        return 0

    lax.fori_loop(0, rows * maps // TILE, fill_cross, 0)

    def fill_slots():
        tiles = tiles_ref[...]
        holders = iota((blk, rows), 0)
        named = (holders == tiles).astype(f32).astype(bf16)
        holds = (iota((blk, blk), 0) == owner_ref[...]).astype(f32).astype(bf16)
        hot = jnp.dot(holds, named, preferred_element_type=f32)
        dest = jnp.sum(holders.astype(f32) * hot, axis=0, keepdims=True).astype(jnp.int32)
        upto = (iota((rows, rows), 0) <= iota((rows, rows), 1)).astype(f32).astype(bf16)
        counts = jnp.dot(hot.astype(bf16), upto, preferred_element_type=f32)
        rank = jnp.sum(counts * hot, axis=0, keepdims=True).astype(jnp.int32) - 1
        slot = dest * cap + rank
        spot = iota((rows, rows), 1)
        spot = 2 * lax.rem(spot, half_rows) + lax.div(spot, half_rows)
        order = (iota((rows, rows), 0) == spot).astype(f32).astype(bf16)
        for i in range(slots // LANES):
            at = i * LANES + iota((LANES, rows), 0)
            hits = (at == slot).astype(f32).astype(bf16)
            slot_hot[i * LANES:(i + 1) * LANES, :] = jnp.dot(
                hits, order, preferred_element_type=f32).astype(bf16)
        place = lax.rem(me, LANES // cap) * cap + rank
        marks = jnp.where(iota((LANES, rows), 0) == place, (offs_ref[...] + 1).astype(f32), 0.0)
        table = lax.dot_general(
            hot.astype(bf16), marks.astype(bf16), (((1,), (1,)), ((), ())),
            preferred_element_type=f32)
        for d in range(blk):
            o_send[d] = table[d:d + 1, :]
        o_recv[me] = o_send[me]

        def send(i, _):
            to = lax.rem(me + i, blk)
            pltpu.make_async_remote_copy(
                src_ref=o_send.at[to], dst_ref=o_recv.at[me], send_sem=os_sem,
                recv_sem=or_sem, device_id=(to, my_map), device_id_type=mesh_id).start()
            return 0

        lax.fori_loop(1, blk, send, 0)

    for copy in inputs[1:]:
        copy.wait()
    fill_slots()

    def order_weights(i, _):
        at = pl.ds(pl.multiple_of(i * LANES, LANES), LANES)
        r = i * LANES + iota((LANES, columns), 0)
        r = 2 * lax.rem(r, columns // 2) + lax.div(r, columns // 2)
        order = (iota((LANES, columns), 1) == r).astype(f32).astype(bf16)
        weights[at, :] = jnp.dot(
            order, weight_ref[...], preferred_element_type=f32).astype(bf16)
        return 0

    lax.fori_loop(0, chunks, order_weights, 0)

    def fill_trig(i, _):
        at = pl.ds(pl.multiple_of(lax.rem(i, pulses // TILE) * TILE, TILE), TILE)
        k = lax.div(i, pulses // TILE)
        q = (k * maps + my_map) * pulses + lax.rem(i, pulses // TILE) * TILE + iota((TILE, 1), 0)
        s = q.astype(f32) * (1.0 / span) - 0.5
        r = iota((TILE, freqs), 1).astype(f32) * (1.0 / freqs) - 0.5
        angle = curv_ref[0] * (s * s) * (1.0 + r)
        c, si = cos_sin_turns(angle * (0.5 / math.pi))
        trig[k, 0, at, :] = c
        trig[k, 1, at, :] = si
        return 0

    lax.fori_loop(0, STOPS * pulses // TILE, fill_trig, 0)

    def turned(k, i):
        at = pl.ds(pl.multiple_of(i * TILE, TILE), TILE)
        c, si = trig[k, 0, at, :], trig[k, 1, at, :]
        re = blocks[k, at, 0:freqs].astype(f32)
        im = blocks[k, at, freqs:2 * freqs].astype(f32)
        return re * c - im * si, re * si + im * c

    def phase(j):
        def turn(i, _):
            first = turned(j, i)
            second = turned(j + STOPS // 2, i)
            for part in range(2):
                z_sum, z_diff = first[part] + second[part], first[part] - second[part]
                to = slice(part * half_freqs, (part + 1) * half_freqs)
                for odd_row, z in ((0, z_sum), (1, z_diff)):
                    at = pl.ds(pl.multiple_of(odd_row * pulses + i * TILE, TILE), TILE)
                    near, far = z[:, :half_freqs], z[:, half_freqs:]
                    phased[0, at, to] = (near + far).astype(bf16)
                    phased[1, at, to] = (near - far).astype(bf16)
            return 0

        lax.fori_loop(0, pulses // TILE, turn, 0, unroll=2)

    def spectrum(j, n):
        top = pl.ds(pl.multiple_of(j * pulses, pulses), pulses)
        low = pl.ds(pl.multiple_of(stacked + j * pulses, pulses), pulses)
        odd = lax.div(n, half_chunks)
        y = jnp.dot(phased[odd], ranges[n], preferred_element_type=f32)
        yr, yi = y[:, :LANES], y[:, LANES:]
        for odd_row in range(2):
            cut = slice(odd_row * pulses, (odd_row + 1) * pulses)
            real, imag = yr[cut].astype(bf16), yi[cut].astype(bf16)
            right[n, odd_row, top, 0:LANES] = real
            right[n, odd_row, top, LANES:width] = imag
            right[n, odd_row, low, 0:LANES] = (-yi[cut]).astype(bf16)
            right[n, odd_row, low, LANES:width] = real

    def near(stop):
        pass_on(stop, stop + shift, partner, jnp.where(stop == 5, 5, 6))

    near_stop = jnp.where(quad < 2, 5, 1)

    def step(i, _):
        j = jnp.where(i == 0, 3, jnp.where(i == 1, 2 * core, 1 - core))

        @pl.when(i == 0)
        def _():
            near(near_stop)

            @pl.when(quad == 1)
            def _():
                pass_on(7, 5, device(me + 2), 8)

            @pl.when(quad == 2)
            def _():
                pass_on(0, 1, device(me - 1), 9)

            @pl.when(core == 0)
            def _():
                pass_on(7, 6, partner, 7)

            @pl.when(quad == 3)
            def _():
                arrived_block(7)

        @pl.when(i == 1 + core)
        def _():
            near(6 - near_stop)

        @pl.when((j == 0) & (quad != 2))
        def _():
            arrived_block(0)

        @pl.when((j == 0) | (j == 2))
        def _():
            arrived_block(jnp.maximum(j, 0) + STOPS // 2)

        @pl.when(j == 2)
        def _():
            arrived_block(2)

        phase(j)
        for n in range(chunks):
            spectrum(j, n)
        return 0

    lax.fori_loop(0, STOPS // 2 - 1, step, 0)

    @pl.when(core == 0)
    def _():
        arrived_block(2)
        arrived_block(6)

    phase(last)
    first_parts = 2
    parts = chunks + first_parts - 1

    def part_of(s):
        if s < first_parts:
            return 0, pl.ds(s * LANES, LANES), slice(s * LANES, (s + 1) * LANES)
        return s - first_parts + 1, pl.ds(0, width), slice(0, width)

    def x_copy(s):
        n, lanes, _ = part_of(s)
        return pltpu.make_async_remote_copy(
            src_ref=x_send.at[n, :, lanes], dst_ref=x_recv.at[n, :, lanes], send_sem=xs_sem.at[s],
            recv_sem=xr_sem.at[s], device_id=(me, other_map), device_id_type=mesh_id)

    own_slots = pl.ds(pl.multiple_of(me * cap, cap), cap)

    def produce(n):
        spectrum(last, n)
        for odd_row in range(2):
            table = cross[odd_row * rows:(odd_row + 1) * rows, :]
            y = jnp.dot(table, right[n, odd_row], preferred_element_type=f32)
            to = slice(odd_row * half_rows, (odd_row + 1) * half_rows)
            x_send[n, to, :] = y[:half_rows].astype(bf16)
            x_own[n, to, :] = y[half_rows:]
        for s in range(parts):
            if part_of(s)[0] == n:
                x_copy(s).start()

    def route(s):
        n, lanes, cut = part_of(s)
        x_copy(s).wait_recv()
        image = (x_own[n, :, cut] + x_recv[n, :, cut].astype(f32)).astype(bf16)
        packed[n, :, cut] = jnp.dot(
            slot_hot[...], image, preferred_element_type=f32).astype(bf16)

        def send(i, _):
            to = lax.rem(me + i, blk)
            pltpu.make_async_remote_copy(
                src_ref=packed.at[n, pl.ds(pl.multiple_of(to * cap, cap), cap), lanes],
                dst_ref=arrived.at[n, own_slots, lanes], send_sem=as_sem.at[s],
                recv_sem=ar_sem.at[s], device_id=(to, my_map),
                device_id_type=mesh_id).start()
            return 0

        lax.fori_loop(1, blk, send, 0)
        arrived[n, own_slots, cut] = packed[n, own_slots, cut]

    produce(0)
    for s in range(parts):
        n = part_of(s)[0]
        if (s == 0 or part_of(s - 1)[0] != n) and n + 1 < chunks:
            produce(n + 1)
        route(s)

    def wait_bytes(ref, sem):
        pltpu.make_async_copy(ref, ref, sem).wait()

    others = pl.ds(0, (blk - 1) * cap)

    accs = ((u_acc, 0), (v_acc, LANES))

    def product(n, at, cut):
        return jnp.dot(
            arrived[n, cut, at:at + LANES], weights[n * LANES:(n + 1) * LANES, :],
            preferred_element_type=f32)

    every = slice(0, slots)

    def interp(s):
        n, lanes, cut = part_of(s)
        wait_bytes(arrived.at[n, others, lanes], ar_sem.at[s])
        for acc, at in accs:
            if not cut.start <= at < cut.stop:
                continue
            if n == 0:
                acc[...] = product(n, at, every)
            elif n < chunks - 1:
                acc[...] += product(n, at, every)
            elif s < parts - 1:
                acc[...] += product(n, at, every)

    for s in range(parts):
        interp(s)
    final = part_of(parts - 1)[2]
    wait_bytes(o_recv.at[pl.ds(0, blk - 1)], or_sem)
    per = LANES // cap
    pieces = []
    for g in range(blk // per):
        total = o_recv[g * per]
        for j in range(1, per):
            total = total + o_recv[g * per + j]
        pieces.append(total)
    total = jnp.zeros((MAPH, columns), f32)
    group = 2 * LANES if slots % (2 * LANES) == 0 else LANES
    for g in range(slots // group):
        cut = slice(g * group, (g + 1) * group)
        spot = jnp.concatenate([
            (iota((MAPH, LANES), 0) == pieces[k].astype(jnp.int32) - 1).astype(f32)
            for k in range(g * group // LANES, (g + 1) * group // LANES)], axis=1).astype(bf16)
        power = 0.0
        for acc, at in accs:
            value = acc[cut, :]
            if chunks > 1 and final.start <= at < final.stop:
                value = value + product(chunks - 1, at, cut)
            power = power + value * value
        high = power.astype(bf16)
        mid = (power - high.astype(f32)).astype(bf16)
        for part in (high, mid):
            total = total + jnp.dot(spot, part, preferred_element_type=f32)
    out_ref[...] = total

    def sent(kind):
        for h in range(2):
            wait_bytes(half_of(0, h), g_send.at[kind, h])

    for kind in (0, 4, 5, 6):
        sent(kind)
    for kind, used in (
            (1, core == 1), (2, quad != 1), (3, quad != 3), (7, core == 0), (8, quad == 1), (9, quad == 2)):
        pl.when(used)(functools.partial(sent, kind))
    for s in range(parts):
        n, lanes, _ = part_of(s)
        wait_bytes(x_send.at[n, :, lanes], xs_sem.at[s])
        wait_bytes(packed.at[n, others, lanes], as_sem.at[s])
    wait_bytes(o_send.at[pl.ds(0, blk - 1)], os_sem)


def body(phase_history, tile_curvature, interp_weights, strip_tiles, row_offsets, tile_owner):
    blk = lax.axis_size("blk")
    maps = lax.axis_size("map")
    pulses = phase_history.shape[2]
    freqs = phase_history.shape[3] // 2
    columns = interp_weights.shape[2]
    rows = strip_tiles.shape[2]
    cap = max(TILE, 2 * rows // blk)
    slots = blk * cap
    chunks = columns // LANES
    width = 2 * LANES
    stacked = STOPS // 2 * pulses
    f32, bf16 = jnp.float32, jnp.bfloat16
    hbm = pl.BlockSpec(memory_space=pltpu.HBM)
    vmem = pl.BlockSpec(memory_space=pltpu.VMEM)
    dma = pltpu.SemaphoreType.DMA
    in_hbm = functools.partial(pltpu.with_memory_space_constraint, memory_space=pltpu.HBM)
    out = pl.pallas_call(
        functools.partial(kernel, (blk, maps, pulses, freqs, columns, rows, cap)),
        out_shape=jax.ShapeDtypeStruct((MAPH, columns), f32),
        in_specs=[hbm, pl.BlockSpec(memory_space=pltpu.SMEM), hbm, hbm, hbm, hbm],
        out_specs=vmem,
        scratch_shapes=[
            pltpu.VMEM((columns, columns), bf16),
            pltpu.VMEM((1, rows), jnp.int32),
            pltpu.VMEM((1, rows), jnp.int32),
            pltpu.VMEM((1, blk), jnp.int32),
            dma((5,)),
            pltpu.VMEM((STOPS, 2, pulses, freqs), f32),
            pltpu.VMEM((STOPS, pulses, 2 * freqs), bf16),
            pltpu.VMEM((chunks, freqs, width), bf16),
            pltpu.VMEM((rows * maps, 2 * stacked), bf16),
            pltpu.VMEM((2, 2 * pulses, freqs), bf16),
            pltpu.VMEM((chunks, 2, 2 * stacked, width), bf16),
            pltpu.VMEM((columns, columns), bf16),
            pltpu.VMEM((chunks, rows, width), bf16),
            pltpu.VMEM((chunks, rows, width), bf16),
            pltpu.VMEM((chunks, rows, width), f32),
            pltpu.VMEM((chunks, slots, width), bf16),
            pltpu.VMEM((chunks, slots, width), bf16),
            pltpu.VMEM((slots, rows), bf16),
            pltpu.VMEM((blk, 1, LANES), f32),
            pltpu.VMEM((blk, 1, LANES), f32),
            pltpu.VMEM((slots, columns), f32),
            pltpu.VMEM((slots, columns), f32),
            dma((10, 2)), dma((STOPS, 2)), dma((chunks + 1,)), dma((chunks + 1,)),
            dma((chunks + 1,)), dma((chunks + 1,)), dma, dma,
        ],
        compiler_params=pltpu.CompilerParams(
            collective_id=0, has_side_effects=True, vmem_limit_bytes=40 * 2**20),
    )(
        in_hbm(phase_history[0, 0]), tile_curvature, in_hbm(interp_weights[0]),
        in_hbm(strip_tiles[0, 0].reshape(1, rows)), in_hbm(row_offsets[0]),
        in_hbm(tile_owner.reshape(1, blk)),
    )
    return jnp.maximum(out, 0.0).reshape(1, 1, MAPH, columns)


def solution(mesh):
    in_specs = (
        P("blk", "map", None, None),
        P("blk"),
        P("blk", None, None),
        P("blk", "map", None, None),
        P("blk", "map", None),
        P(),
    )
    out_specs = P("blk", "map", None, None)
    return jax.shard_map(body, mesh=mesh, in_specs=in_specs, out_specs=out_specs, check_vma=False)
```

```python
import functools
import math

import jax
import jax.numpy as jnp
import numpy as np
from jax import lax
from jax.experimental import pallas as pl
from jax.experimental.pallas import tpu as pltpu
from jax.sharding import PartitionSpec as P

STOPS = 8
MAPH = 256
LANES = 128
TILE = 16


def fit_turns():
    z = 0.125 - 0.125 * np.cos(np.pi * (np.arange(400) + 0.5) / 400)
    t = np.sqrt(z)
    cheb = np.polynomial.chebyshev.Chebyshev
    cos_fit = cheb.fit(z, np.cos(2 * np.pi * t), 7, domain=[0, 0.25])
    sin_fit = cheb.fit(z, np.sin(2 * np.pi * t) / t, 6, domain=[0, 0.25])
    power = np.polynomial.Polynomial
    return (
        [float(np.float32(c)) for c in cos_fit.convert(kind=power).coef],
        [float(np.float32(c)) for c in sin_fit.convert(kind=power).coef],
    )


COS_COEF, SIN_COEF = fit_turns()


def cos_sin_turns(turns):
    t = turns - jnp.round(turns)
    z = t * t
    c = jnp.full_like(z, COS_COEF[-1])
    for coef in COS_COEF[-2::-1]:
        c = c * z + coef
    s = jnp.full_like(z, SIN_COEF[-1])
    for coef in SIN_COEF[-2::-1]:
        s = s * z + coef
    return c, s * t


def iota(shape, axis):
    return lax.broadcasted_iota(jnp.int32, shape, axis)


def kernel(
    sizes,
    block_hbm, curv_ref, weight_hbm, tiles_hbm, offs_hbm, owner_hbm,
    out_ref,
    weight_ref, tiles_ref, offs_ref, owner_ref, in_sem, trig, blocks, ranges, cross, phased, right, weights, x_send, x_recv, x_own, packed, arrived, slot_hot,
    o_send, o_recv, u_acc, v_acc,
    g_send, g_recv, xs_sem, xr_sem, as_sem, ar_sem, os_sem, or_sem,
):
    blk, maps, pulses, freqs, columns, rows, cap = sizes
    f32, bf16 = jnp.float32, jnp.bfloat16
    me = lax.axis_index("blk")
    my_map = lax.axis_index("map")
    other_map = 1 - my_map
    core = lax.rem(me, 2)
    span = STOPS * maps * pulses
    stacked = STOPS // 2 * pulses
    chunks = columns // LANES
    width = 2 * LANES
    slots = blk * cap
    own_stop = STOPS // 2 - 1

    def device(index):
        return (lax.rem(index + 2 * blk, blk), my_map)

    mesh_id = pl.DeviceIdType.MESH

    barrier = pltpu.get_barrier_semaphore()

    def greet(i, _):
        pl.semaphore_signal(barrier, inc=1, device_id=device(me + i), device_id_type=mesh_id)
        return 0

    lax.fori_loop(1, blk, greet, 0)
    pl.semaphore_signal(barrier, inc=1, device_id=(me, other_map), device_id_type=mesh_id)

    def bring(source, target, sem):
        return pltpu.make_async_copy(source, target, in_sem.at[sem])

    inputs = [
        bring(block_hbm, blocks.at[own_stop], 0),
        bring(owner_hbm, owner_ref, 1),
        bring(tiles_hbm, tiles_ref, 2),
        bring(offs_hbm, offs_ref, 3),
        bring(weight_hbm, weight_ref, 4),
    ]
    for copy in inputs:
        copy.start()
    inputs[0].wait()
    pl.semaphore_wait(barrier, blk)

    partner = device(me + 1 - 2 * core)
    shift = 2 * core - 1
    quad = lax.rem(me, 4)
    half = pulses // 2
    last = 2 - core

    def half_of(stop, h):
        return blocks.at[stop, pl.ds(h * half, half)]

    def push(source, stop, h, target, kind):
        pltpu.make_async_remote_copy(
            src_ref=half_of(source, h), dst_ref=half_of(stop, h), send_sem=g_send.at[kind, h],
            recv_sem=g_recv.at[stop, h], device_id=target, device_id_type=mesh_id).start()

    def push_own(stop, target, kind):
        for h in range(2):
            push(own_stop, stop, h, target, kind)

    def arrived_half(stop, h):
        pltpu.make_async_copy(half_of(stop, h), half_of(stop, h), g_recv.at[stop, h]).wait()

    def arrived_block(stop):
        for h in range(2):
            arrived_half(stop, h)

    def pass_on(stop, to_stop, target, kind):
        for h in range(2):
            arrived_half(stop, h)
            push(stop, to_stop, h, target, kind)

    @pl.when(quad == 3)
    def _():
        push_own(0, device(me + 3), 1)

    push_own(7, device(me - 4), 0)

    @pl.when(quad == 1)
    def _():
        push_own(0, device(me + 3), 1)

    @pl.when(quad != 1)
    def _():
        push_own(5, device(me - 2), 2)

    @pl.when(quad != 3)
    def _():
        push_own(1, device(me + 2), 3)

    push_own(own_stop + shift, partner, 4)

    half_freqs = freqs // 2
    half_chunks = chunks // 2
    half_rows = rows // 2

    def fill_ranges(i, _):
        at = pl.ds(pl.multiple_of(i * TILE, TILE), TILE)
        below = pl.ds(pl.multiple_of(half_freqs + i * TILE, TILE), TILE)
        f = (i * TILE + iota((TILE, columns // 2), 0)).astype(f32)
        for odd in range(2):
            c = (2 * iota((TILE, columns // 2), 1) + odd).astype(f32)
            re, im = cos_sin_turns(f * c * (1.0 / freqs))
            re = (re * (1.0 / math.sqrt(freqs))).astype(bf16)
            im = (im * (1.0 / math.sqrt(freqs)))
            pos, neg = im.astype(bf16), (-im).astype(bf16)
            for n in range(half_chunks):
                cut = slice(n * LANES, (n + 1) * LANES)
                to = odd * half_chunks + n
                ranges[to, at, 0:LANES] = re[:, cut]
                ranges[to, at, LANES:width] = neg[:, cut]
                ranges[to, below, 0:LANES] = pos[:, cut]
                ranges[to, below, LANES:width] = re[:, cut]
        return 0

    lax.fori_loop(0, half_freqs // TILE, fill_ranges, 0)

    lane = iota((1, stacked), 1)
    q_lane = (lane + (lax.div(lane, pulses) * (maps - 1) + my_map) * pulses).astype(f32)

    def fill_cross(i, _):
        at = pl.ds(pl.multiple_of(i * TILE, TILE), TILE)
        g = i * TILE
        odd = lax.div(g, rows)
        own = lax.div(lax.rem(g, rows), half_rows)
        part = jnp.where(own == 1, my_map, other_map)
        base = part * rows + odd + 2 * lax.rem(g, half_rows)
        a = (base + 2 * iota((TILE, stacked), 0)).astype(f32)
        re, im = cos_sin_turns(a * q_lane * (1.0 / span))
        cross[at, 0:stacked] = (re * (1.0 / math.sqrt(span))).astype(bf16)
        cross[at, stacked:2 * stacked] = (im * (-1.0 / math.sqrt(span))).astype(bf16)
        return 0

    lax.fori_loop(0, rows * maps // TILE, fill_cross, 0)

    def fill_slots():
        tiles = tiles_ref[...]
        holders = iota((blk, rows), 0)
        named = (holders == tiles).astype(f32).astype(bf16)
        holds = (iota((blk, blk), 0) == owner_ref[...]).astype(f32).astype(bf16)
        hot = jnp.dot(holds, named, preferred_element_type=f32)
        dest = jnp.sum(holders.astype(f32) * hot, axis=0, keepdims=True).astype(jnp.int32)
        upto = (iota((rows, rows), 0) <= iota((rows, rows), 1)).astype(f32).astype(bf16)
        counts = jnp.dot(hot.astype(bf16), upto, preferred_element_type=f32)
        rank = jnp.sum(counts * hot, axis=0, keepdims=True).astype(jnp.int32) - 1
        slot = dest * cap + rank
        spot = iota((rows, rows), 1)
        spot = 2 * lax.rem(spot, half_rows) + lax.div(spot, half_rows)
        order = (iota((rows, rows), 0) == spot).astype(f32).astype(bf16)
        for i in range(slots // LANES):
            at = i * LANES + iota((LANES, rows), 0)
            hits = (at == slot).astype(f32).astype(bf16)
            slot_hot[i * LANES:(i + 1) * LANES, :] = jnp.dot(
                hits, order, preferred_element_type=f32).astype(bf16)
        place = lax.rem(me, LANES // cap) * cap + rank
        marks = jnp.where(iota((LANES, rows), 0) == place, (offs_ref[...] + 1).astype(f32), 0.0)
        table = lax.dot_general(
            hot.astype(bf16), marks.astype(bf16), (((1,), (1,)), ((), ())),
            preferred_element_type=f32)
        for d in range(blk):
            o_send[d] = table[d:d + 1, :]
        o_recv[me] = o_send[me]

        def send(i, _):
            to = lax.rem(me + i, blk)
            pltpu.make_async_remote_copy(
                src_ref=o_send.at[to], dst_ref=o_recv.at[me], send_sem=os_sem,
                recv_sem=or_sem, device_id=(to, my_map), device_id_type=mesh_id).start()
            return 0

        lax.fori_loop(1, blk, send, 0)

    for copy in inputs[1:]:
        copy.wait()
    fill_slots()

    def order_weights(i, _):
        at = pl.ds(pl.multiple_of(i * LANES, LANES), LANES)
        r = i * LANES + iota((LANES, columns), 0)
        r = 2 * lax.rem(r, columns // 2) + lax.div(r, columns // 2)
        order = (iota((LANES, columns), 1) == r).astype(f32).astype(bf16)
        weights[at, :] = jnp.dot(
            order, weight_ref[...], preferred_element_type=f32).astype(bf16)
        return 0

    lax.fori_loop(0, chunks, order_weights, 0)

    def fill_trig(i, _):
        at = pl.ds(pl.multiple_of(lax.rem(i, pulses // TILE) * TILE, TILE), TILE)
        k = lax.div(i, pulses // TILE)
        q = (k * maps + my_map) * pulses + lax.rem(i, pulses // TILE) * TILE + iota((TILE, 1), 0)
        s = q.astype(f32) * (1.0 / span) - 0.5
        r = iota((TILE, freqs), 1).astype(f32) * (1.0 / freqs) - 0.5
        angle = curv_ref[0] * (s * s) * (1.0 + r)
        c, si = cos_sin_turns(angle * (0.5 / math.pi))
        trig[k, 0, at, :] = c
        trig[k, 1, at, :] = si
        return 0

    lax.fori_loop(0, STOPS * pulses // TILE, fill_trig, 0)

    def turned(k, i):
        at = pl.ds(pl.multiple_of(i * TILE, TILE), TILE)
        c, si = trig[k, 0, at, :], trig[k, 1, at, :]
        re = blocks[k, at, 0:freqs].astype(f32)
        im = blocks[k, at, freqs:2 * freqs].astype(f32)
        return re * c - im * si, re * si + im * c

    def phase(j):
        def turn(i, _):
            first = turned(j, i)
            second = turned(j + STOPS // 2, i)
            for part in range(2):
                z_sum, z_diff = first[part] + second[part], first[part] - second[part]
                to = slice(part * half_freqs, (part + 1) * half_freqs)
                for odd_row, z in ((0, z_sum), (1, z_diff)):
                    at = pl.ds(pl.multiple_of(odd_row * pulses + i * TILE, TILE), TILE)
                    near, far = z[:, :half_freqs], z[:, half_freqs:]
                    phased[0, at, to] = (near + far).astype(bf16)
                    phased[1, at, to] = (near - far).astype(bf16)
            return 0

        lax.fori_loop(0, pulses // TILE, turn, 0, unroll=2)

    def spectrum(j, n):
        top = pl.ds(pl.multiple_of(j * pulses, pulses), pulses)
        low = pl.ds(pl.multiple_of(stacked + j * pulses, pulses), pulses)
        odd = lax.div(n, half_chunks)
        y = jnp.dot(phased[odd], ranges[n], preferred_element_type=f32)
        yr, yi = y[:, :LANES], y[:, LANES:]
        for odd_row in range(2):
            cut = slice(odd_row * pulses, (odd_row + 1) * pulses)
            real, imag = yr[cut].astype(bf16), yi[cut].astype(bf16)
            right[n, odd_row, top, 0:LANES] = real
            right[n, odd_row, top, LANES:width] = imag
            right[n, odd_row, low, 0:LANES] = (-yi[cut]).astype(bf16)
            right[n, odd_row, low, LANES:width] = real

    def near(stop):
        pass_on(stop, stop + shift, partner, jnp.where(stop == 5, 5, 6))

    near_stop = jnp.where(quad < 2, 5, 1)

    def step(i, _):
        j = jnp.where(i == 0, 3, jnp.where(i == 1, 2 * core, 1 - core))

        @pl.when(i == 0)
        def _():
            near(near_stop)

            @pl.when(quad == 1)
            def _():
                pass_on(7, 5, device(me + 2), 8)

            @pl.when(quad == 2)
            def _():
                pass_on(0, 1, device(me - 1), 9)

            @pl.when(core == 0)
            def _():
                pass_on(7, 6, partner, 7)

            @pl.when(quad == 3)
            def _():
                arrived_block(7)

        @pl.when(i == 1 + core)
        def _():
            near(6 - near_stop)

        @pl.when((j == 0) & (quad != 2))
        def _():
            arrived_block(0)

        @pl.when((j == 0) | (j == 2))
        def _():
            arrived_block(jnp.maximum(j, 0) + STOPS // 2)

        @pl.when(j == 2)
        def _():
            arrived_block(2)

        phase(j)
        for n in range(chunks):
            spectrum(j, n)
        return 0

    lax.fori_loop(0, STOPS // 2 - 1, step, 0)

    @pl.when(core == 0)
    def _():
        arrived_block(2)
        arrived_block(6)

    phase(last)
    first_parts = 2
    parts = chunks + first_parts - 1

    def part_of(s):
        if s < first_parts:
            return 0, pl.ds(s * LANES, LANES), slice(s * LANES, (s + 1) * LANES)
        return s - first_parts + 1, pl.ds(0, width), slice(0, width)

    def x_copy(s):
        n, lanes, _ = part_of(s)
        return pltpu.make_async_remote_copy(
            src_ref=x_send.at[n, :, lanes], dst_ref=x_recv.at[n, :, lanes], send_sem=xs_sem.at[s],
            recv_sem=xr_sem.at[s], device_id=(me, other_map), device_id_type=mesh_id)

    own_slots = pl.ds(pl.multiple_of(me * cap, cap), cap)

    def produce(n):
        spectrum(last, n)
        for odd_row in range(2):
            table = cross[odd_row * rows:(odd_row + 1) * rows, :]
            y = jnp.dot(table, right[n, odd_row], preferred_element_type=f32)
            to = slice(odd_row * half_rows, (odd_row + 1) * half_rows)
            x_send[n, to, :] = y[:half_rows].astype(bf16)
            x_own[n, to, :] = y[half_rows:]
        for s in range(parts):
            if part_of(s)[0] == n:
                x_copy(s).start()

    def route(s):
        n, lanes, cut = part_of(s)
        x_copy(s).wait_recv()
        image = (x_own[n, :, cut] + x_recv[n, :, cut].astype(f32)).astype(bf16)
        packed[n, :, cut] = jnp.dot(
            slot_hot[...], image, preferred_element_type=f32).astype(bf16)

        def send(i, _):
            to = jnp.where(i - 1 < me, i - 1, i) if s == parts - 1 else lax.rem(me + i, blk)
            pltpu.make_async_remote_copy(
                src_ref=packed.at[n, pl.ds(pl.multiple_of(to * cap, cap), cap), lanes],
                dst_ref=arrived.at[n, own_slots, lanes], send_sem=as_sem.at[s],
                recv_sem=ar_sem.at[s], device_id=(to, my_map),
                device_id_type=mesh_id).start()
            return 0

        lax.fori_loop(1, blk, send, 0)
        arrived[n, own_slots, cut] = packed[n, own_slots, cut]

    produce(0)
    for s in range(parts):
        n = part_of(s)[0]
        if (s == 0 or part_of(s - 1)[0] != n) and n + 1 < chunks:
            produce(n + 1)
        route(s)

    def wait_bytes(ref, sem):
        pltpu.make_async_copy(ref, ref, sem).wait()

    others = pl.ds(0, (blk - 1) * cap)

    accs = ((u_acc, 0), (v_acc, LANES))

    def product(n, at, cut):
        return jnp.dot(
            arrived[n, cut, at:at + LANES], weights[n * LANES:(n + 1) * LANES, :],
            preferred_element_type=f32)

    every = slice(0, slots)

    def interp(s):
        n, lanes, cut = part_of(s)
        wait_bytes(arrived.at[n, others, lanes], ar_sem.at[s])
        for acc, at in accs:
            if not cut.start <= at < cut.stop:
                continue
            if n == 0:
                acc[...] = product(n, at, every)
            elif n < chunks - 1:
                acc[...] += product(n, at, every)
            elif s < parts - 1:
                acc[...] += product(n, at, every)

    for s in range(parts):
        interp(s)
    final = part_of(parts - 1)[2]
    wait_bytes(o_recv.at[pl.ds(0, blk - 1)], or_sem)
    per = LANES // cap
    pieces = []
    for g in range(blk // per):
        total = o_recv[g * per]
        for j in range(1, per):
            total = total + o_recv[g * per + j]
        pieces.append(total)
    total = jnp.zeros((MAPH, columns), f32)
    group = 2 * LANES if slots % (2 * LANES) == 0 else LANES
    for g in range(slots // group):
        cut = slice(g * group, (g + 1) * group)
        spot = jnp.concatenate([
            (iota((MAPH, LANES), 0) == pieces[k].astype(jnp.int32) - 1).astype(f32)
            for k in range(g * group // LANES, (g + 1) * group // LANES)], axis=1).astype(bf16)
        power = 0.0
        for acc, at in accs:
            value = acc[cut, :]
            if chunks > 1 and final.start <= at < final.stop:
                value = value + product(chunks - 1, at, cut)
            power = power + value * value
        high = power.astype(bf16)
        mid = (power - high.astype(f32)).astype(bf16)
        for part in (high, mid):
            total = total + jnp.dot(spot, part, preferred_element_type=f32)
    out_ref[...] = total

    def sent(kind):
        for h in range(2):
            wait_bytes(half_of(0, h), g_send.at[kind, h])

    for kind in (0, 4, 5, 6):
        sent(kind)
    for kind, used in (
            (1, core == 1), (2, quad != 1), (3, quad != 3), (7, core == 0), (8, quad == 1), (9, quad == 2)):
        pl.when(used)(functools.partial(sent, kind))
    for s in range(parts):
        n, lanes, _ = part_of(s)
        wait_bytes(x_send.at[n, :, lanes], xs_sem.at[s])
        wait_bytes(packed.at[n, others, lanes], as_sem.at[s])
    wait_bytes(o_send.at[pl.ds(0, blk - 1)], os_sem)


def body(phase_history, tile_curvature, interp_weights, strip_tiles, row_offsets, tile_owner):
    blk = lax.axis_size("blk")
    maps = lax.axis_size("map")
    pulses = phase_history.shape[2]
    freqs = phase_history.shape[3] // 2
    columns = interp_weights.shape[2]
    rows = strip_tiles.shape[2]
    cap = max(TILE, 2 * rows // blk)
    slots = blk * cap
    chunks = columns // LANES
    width = 2 * LANES
    stacked = STOPS // 2 * pulses
    f32, bf16 = jnp.float32, jnp.bfloat16
    hbm = pl.BlockSpec(memory_space=pltpu.HBM)
    vmem = pl.BlockSpec(memory_space=pltpu.VMEM)
    dma = pltpu.SemaphoreType.DMA
    in_hbm = functools.partial(pltpu.with_memory_space_constraint, memory_space=pltpu.HBM)
    out = pl.pallas_call(
        functools.partial(kernel, (blk, maps, pulses, freqs, columns, rows, cap)),
        out_shape=jax.ShapeDtypeStruct((MAPH, columns), f32),
        in_specs=[hbm, pl.BlockSpec(memory_space=pltpu.SMEM), hbm, hbm, hbm, hbm],
        out_specs=vmem,
        scratch_shapes=[
            pltpu.VMEM((columns, columns), bf16),
            pltpu.VMEM((1, rows), jnp.int32),
            pltpu.VMEM((1, rows), jnp.int32),
            pltpu.VMEM((1, blk), jnp.int32),
            dma((5,)),
            pltpu.VMEM((STOPS, 2, pulses, freqs), f32),
            pltpu.VMEM((STOPS, pulses, 2 * freqs), bf16),
            pltpu.VMEM((chunks, freqs, width), bf16),
            pltpu.VMEM((rows * maps, 2 * stacked), bf16),
            pltpu.VMEM((2, 2 * pulses, freqs), bf16),
            pltpu.VMEM((chunks, 2, 2 * stacked, width), bf16),
            pltpu.VMEM((columns, columns), bf16),
            pltpu.VMEM((chunks, rows, width), bf16),
            pltpu.VMEM((chunks, rows, width), bf16),
            pltpu.VMEM((chunks, rows, width), f32),
            pltpu.VMEM((chunks, slots, width), bf16),
            pltpu.VMEM((chunks, slots, width), bf16),
            pltpu.VMEM((slots, rows), bf16),
            pltpu.VMEM((blk, 1, LANES), f32),
            pltpu.VMEM((blk, 1, LANES), f32),
            pltpu.VMEM((slots, columns), f32),
            pltpu.VMEM((slots, columns), f32),
            dma((10, 2)), dma((STOPS, 2)), dma((chunks + 1,)), dma((chunks + 1,)),
            dma((chunks + 1,)), dma((chunks + 1,)), dma, dma,
        ],
        compiler_params=pltpu.CompilerParams(
            collective_id=0, has_side_effects=True, vmem_limit_bytes=40 * 2**20),
    )(
        in_hbm(phase_history[0, 0]), tile_curvature, in_hbm(interp_weights[0]),
        in_hbm(strip_tiles[0, 0].reshape(1, rows)), in_hbm(row_offsets[0]),
        in_hbm(tile_owner.reshape(1, blk)),
    )
    return jnp.maximum(out, 0.0).reshape(1, 1, MAPH, columns)


def solution(mesh):
    in_specs = (
        P("blk", "map", None, None),
        P("blk"),
        P("blk", None, None),
        P("blk", "map", None, None),
        P("blk", "map", None),
        P(),
    )
    out_specs = P("blk", "map", None, None)
    return jax.shard_map(body, mesh=mesh, in_specs=in_specs, out_specs=out_specs, check_vma=False)
```

```python
import functools
import math

import jax
import jax.numpy as jnp
import numpy as np
from jax import lax
from jax.experimental import pallas as pl
from jax.experimental.pallas import tpu as pltpu
from jax.sharding import PartitionSpec as P

STOPS = 8
MAPH = 256
LANES = 128
TILE = 16


def fit_turns():
    z = 0.125 - 0.125 * np.cos(np.pi * (np.arange(400) + 0.5) / 400)
    t = np.sqrt(z)
    cheb = np.polynomial.chebyshev.Chebyshev
    cos_fit = cheb.fit(z, np.cos(2 * np.pi * t), 7, domain=[0, 0.25])
    sin_fit = cheb.fit(z, np.sin(2 * np.pi * t) / t, 6, domain=[0, 0.25])
    power = np.polynomial.Polynomial
    return (
        [float(np.float32(c)) for c in cos_fit.convert(kind=power).coef],
        [float(np.float32(c)) for c in sin_fit.convert(kind=power).coef],
    )


COS_COEF, SIN_COEF = fit_turns()


def cos_sin_turns(turns):
    t = turns - jnp.round(turns)
    z = t * t
    c = jnp.full_like(z, COS_COEF[-1])
    for coef in COS_COEF[-2::-1]:
        c = c * z + coef
    s = jnp.full_like(z, SIN_COEF[-1])
    for coef in SIN_COEF[-2::-1]:
        s = s * z + coef
    return c, s * t


def iota(shape, axis):
    return lax.broadcasted_iota(jnp.int32, shape, axis)


def kernel(
    sizes,
    block_hbm, curv_ref, weight_hbm, tiles_hbm, offs_hbm, owner_hbm,
    out_ref,
    weight_ref, tiles_ref, offs_ref, owner_ref, in_sem, trig, blocks, ranges, cross, phased, right, weights, x_send, x_recv, x_own, packed, arrived, slot_hot,
    o_send, o_recv, u_acc, v_acc, spots,
    g_send, g_recv, xs_sem, xr_sem, as_sem, ar_sem, os_sem, or_sem,
):
    blk, maps, pulses, freqs, columns, rows, cap = sizes
    f32, bf16 = jnp.float32, jnp.bfloat16
    me = lax.axis_index("blk")
    my_map = lax.axis_index("map")
    other_map = 1 - my_map
    core = lax.rem(me, 2)
    span = STOPS * maps * pulses
    stacked = STOPS // 2 * pulses
    chunks = columns // LANES
    width = 2 * LANES
    slots = blk * cap
    own_stop = STOPS // 2 - 1

    def device(index):
        return (lax.rem(index + 2 * blk, blk), my_map)

    mesh_id = pl.DeviceIdType.MESH

    barrier = pltpu.get_barrier_semaphore()

    def greet(i, _):
        pl.semaphore_signal(barrier, inc=1, device_id=device(me + i), device_id_type=mesh_id)
        return 0

    lax.fori_loop(1, blk, greet, 0)
    pl.semaphore_signal(barrier, inc=1, device_id=(me, other_map), device_id_type=mesh_id)

    def bring(source, target, sem):
        return pltpu.make_async_copy(source, target, in_sem.at[sem])

    inputs = [
        bring(block_hbm, blocks.at[own_stop], 0),
        bring(owner_hbm, owner_ref, 1),
        bring(tiles_hbm, tiles_ref, 2),
        bring(offs_hbm, offs_ref, 3),
        bring(weight_hbm, weight_ref, 4),
    ]
    for copy in inputs:
        copy.start()
    inputs[0].wait()
    pl.semaphore_wait(barrier, blk)

    partner = device(me + 1 - 2 * core)
    shift = 2 * core - 1
    quad = lax.rem(me, 4)
    half = pulses // 2
    last = 2 - core

    def half_of(stop, h):
        return blocks.at[stop, pl.ds(h * half, half)]

    def push(source, stop, h, target, kind):
        pltpu.make_async_remote_copy(
            src_ref=half_of(source, h), dst_ref=half_of(stop, h), send_sem=g_send.at[kind, h],
            recv_sem=g_recv.at[stop, h], device_id=target, device_id_type=mesh_id).start()

    def push_own(stop, target, kind):
        for h in range(2):
            push(own_stop, stop, h, target, kind)

    def arrived_half(stop, h):
        pltpu.make_async_copy(half_of(stop, h), half_of(stop, h), g_recv.at[stop, h]).wait()

    def arrived_block(stop):
        for h in range(2):
            arrived_half(stop, h)

    def pass_on(stop, to_stop, target, kind):
        for h in range(2):
            arrived_half(stop, h)
            push(stop, to_stop, h, target, kind)

    @pl.when(quad == 3)
    def _():
        push_own(0, device(me + 3), 1)

    push_own(7, device(me - 4), 0)

    @pl.when(quad == 1)
    def _():
        push_own(0, device(me + 3), 1)

    @pl.when(quad != 1)
    def _():
        push_own(5, device(me - 2), 2)

    @pl.when(quad != 3)
    def _():
        push_own(1, device(me + 2), 3)

    push_own(own_stop + shift, partner, 4)

    half_freqs = freqs // 2
    half_chunks = chunks // 2
    half_rows = rows // 2

    def fill_ranges(i, _):
        at = pl.ds(pl.multiple_of(i * TILE, TILE), TILE)
        below = pl.ds(pl.multiple_of(half_freqs + i * TILE, TILE), TILE)
        f = (i * TILE + iota((TILE, columns // 2), 0)).astype(f32)
        for odd in range(2):
            c = (2 * iota((TILE, columns // 2), 1) + odd).astype(f32)
            re, im = cos_sin_turns(f * c * (1.0 / freqs))
            re = (re * (1.0 / math.sqrt(freqs))).astype(bf16)
            im = (im * (1.0 / math.sqrt(freqs)))
            pos, neg = im.astype(bf16), (-im).astype(bf16)
            for n in range(half_chunks):
                cut = slice(n * LANES, (n + 1) * LANES)
                to = odd * half_chunks + n
                ranges[to, at, 0:LANES] = re[:, cut]
                ranges[to, at, LANES:width] = neg[:, cut]
                ranges[to, below, 0:LANES] = pos[:, cut]
                ranges[to, below, LANES:width] = re[:, cut]
        return 0

    lax.fori_loop(0, half_freqs // TILE, fill_ranges, 0)

    lane = iota((1, stacked), 1)
    q_lane = (lane + (lax.div(lane, pulses) * (maps - 1) + my_map) * pulses).astype(f32)

    def fill_cross(i, _):
        at = pl.ds(pl.multiple_of(i * TILE, TILE), TILE)
        g = i * TILE
        odd = lax.div(g, rows)
        own = lax.div(lax.rem(g, rows), half_rows)
        part = jnp.where(own == 1, my_map, other_map)
        base = part * rows + odd + 2 * lax.rem(g, half_rows)
        a = (base + 2 * iota((TILE, stacked), 0)).astype(f32)
        re, im = cos_sin_turns(a * q_lane * (1.0 / span))
        cross[at, 0:stacked] = (re * (1.0 / math.sqrt(span))).astype(bf16)
        cross[at, stacked:2 * stacked] = (im * (-1.0 / math.sqrt(span))).astype(bf16)
        return 0

    lax.fori_loop(0, rows * maps // TILE, fill_cross, 0)

    def fill_slots():
        tiles = tiles_ref[...]
        holders = iota((blk, rows), 0)
        named = (holders == tiles).astype(f32).astype(bf16)
        holds = (iota((blk, blk), 0) == owner_ref[...]).astype(f32).astype(bf16)
        hot = jnp.dot(holds, named, preferred_element_type=f32)
        dest = jnp.sum(holders.astype(f32) * hot, axis=0, keepdims=True).astype(jnp.int32)
        upto = (iota((rows, rows), 0) <= iota((rows, rows), 1)).astype(f32).astype(bf16)
        counts = jnp.dot(hot.astype(bf16), upto, preferred_element_type=f32)
        rank = jnp.sum(counts * hot, axis=0, keepdims=True).astype(jnp.int32) - 1
        slot = dest * cap + rank
        spot = iota((rows, rows), 1)
        spot = 2 * lax.rem(spot, half_rows) + lax.div(spot, half_rows)
        order = (iota((rows, rows), 0) == spot).astype(f32).astype(bf16)
        for i in range(slots // LANES):
            at = i * LANES + iota((LANES, rows), 0)
            hits = (at == slot).astype(f32).astype(bf16)
            slot_hot[i * LANES:(i + 1) * LANES, :] = jnp.dot(
                hits, order, preferred_element_type=f32).astype(bf16)
        place = lax.rem(me, LANES // cap) * cap + rank
        marks = jnp.where(iota((LANES, rows), 0) == place, (offs_ref[...] + 1).astype(f32), 0.0)
        table = lax.dot_general(
            hot.astype(bf16), marks.astype(bf16), (((1,), (1,)), ((), ())),
            preferred_element_type=f32)
        for d in range(blk):
            o_send[d] = table[d:d + 1, :]
        o_recv[me] = o_send[me]

        def send(i, _):
            to = lax.rem(me + i, blk)
            pltpu.make_async_remote_copy(
                src_ref=o_send.at[to], dst_ref=o_recv.at[me], send_sem=os_sem,
                recv_sem=or_sem, device_id=(to, my_map), device_id_type=mesh_id).start()
            return 0

        lax.fori_loop(1, blk, send, 0)

    for copy in inputs[1:]:
        copy.wait()
    fill_slots()

    def order_weights(i, _):
        at = pl.ds(pl.multiple_of(i * LANES, LANES), LANES)
        r = i * LANES + iota((LANES, columns), 0)
        r = 2 * lax.rem(r, columns // 2) + lax.div(r, columns // 2)
        order = (iota((LANES, columns), 1) == r).astype(f32).astype(bf16)
        weights[at, :] = jnp.dot(
            order, weight_ref[...], preferred_element_type=f32).astype(bf16)
        return 0

    lax.fori_loop(0, chunks, order_weights, 0)

    def fill_trig(i, _):
        at = pl.ds(pl.multiple_of(lax.rem(i, pulses // TILE) * TILE, TILE), TILE)
        k = lax.div(i, pulses // TILE)
        q = (k * maps + my_map) * pulses + lax.rem(i, pulses // TILE) * TILE + iota((TILE, 1), 0)
        s = q.astype(f32) * (1.0 / span) - 0.5
        r = iota((TILE, freqs), 1).astype(f32) * (1.0 / freqs) - 0.5
        angle = curv_ref[0] * (s * s) * (1.0 + r)
        c, si = cos_sin_turns(angle * (0.5 / math.pi))
        trig[k, 0, at, :] = c
        trig[k, 1, at, :] = si
        return 0

    lax.fori_loop(0, STOPS * pulses // TILE, fill_trig, 0)

    def turned(k, i):
        at = pl.ds(pl.multiple_of(i * TILE, TILE), TILE)
        c, si = trig[k, 0, at, :], trig[k, 1, at, :]
        re = blocks[k, at, 0:freqs].astype(f32)
        im = blocks[k, at, freqs:2 * freqs].astype(f32)
        return re * c - im * si, re * si + im * c

    def phase(j):
        def turn(i, _):
            first = turned(j, i)
            second = turned(j + STOPS // 2, i)
            for part in range(2):
                z_sum, z_diff = first[part] + second[part], first[part] - second[part]
                to = slice(part * half_freqs, (part + 1) * half_freqs)
                for odd_row, z in ((0, z_sum), (1, z_diff)):
                    at = pl.ds(pl.multiple_of(odd_row * pulses + i * TILE, TILE), TILE)
                    near, far = z[:, :half_freqs], z[:, half_freqs:]
                    phased[0, at, to] = (near + far).astype(bf16)
                    phased[1, at, to] = (near - far).astype(bf16)
            return 0

        lax.fori_loop(0, pulses // TILE, turn, 0, unroll=2)

    def spectrum(j, n):
        top = pl.ds(pl.multiple_of(j * pulses, pulses), pulses)
        low = pl.ds(pl.multiple_of(stacked + j * pulses, pulses), pulses)
        odd = lax.div(n, half_chunks)
        y = jnp.dot(phased[odd], ranges[n], preferred_element_type=f32)
        yr, yi = y[:, :LANES], y[:, LANES:]
        for odd_row in range(2):
            cut = slice(odd_row * pulses, (odd_row + 1) * pulses)
            real, imag = yr[cut].astype(bf16), yi[cut].astype(bf16)
            right[n, odd_row, top, 0:LANES] = real
            right[n, odd_row, top, LANES:width] = imag
            right[n, odd_row, low, 0:LANES] = (-yi[cut]).astype(bf16)
            right[n, odd_row, low, LANES:width] = real

    def near(stop):
        pass_on(stop, stop + shift, partner, jnp.where(stop == 5, 5, 6))

    near_stop = jnp.where(quad < 2, 5, 1)

    def step(i, _):
        j = jnp.where(i == 0, 3, jnp.where(i == 1, 2 * core, 1 - core))

        @pl.when(i == 0)
        def _():
            near(near_stop)

            @pl.when(quad == 1)
            def _():
                pass_on(7, 5, device(me + 2), 8)

            @pl.when(quad == 2)
            def _():
                pass_on(0, 1, device(me - 1), 9)

            @pl.when(core == 0)
            def _():
                pass_on(7, 6, partner, 7)

            @pl.when(quad == 3)
            def _():
                arrived_block(7)

        @pl.when(i == 1 + core)
        def _():
            near(6 - near_stop)

        @pl.when((j == 0) & (quad != 2))
        def _():
            arrived_block(0)

        @pl.when((j == 0) | (j == 2))
        def _():
            arrived_block(jnp.maximum(j, 0) + STOPS // 2)

        @pl.when(j == 2)
        def _():
            arrived_block(2)

        phase(j)
        for n in range(chunks):
            spectrum(j, n)
        return 0

    lax.fori_loop(0, STOPS // 2 - 1, step, 0)

    @pl.when(core == 0)
    def _():
        arrived_block(2)
        arrived_block(6)

    phase(last)
    first_parts = 2
    parts = chunks + first_parts - 1

    def part_of(s):
        if s < first_parts:
            return 0, pl.ds(s, 1), (s,)
        return s - first_parts + 1, pl.ds(0, 2), (0, 1)

    joined = 2 if chunks >= 4 else 1
    groups = parts - joined + 1

    def group_of(g):
        n, lanes, halves = part_of(g)
        return n, pl.ds(n, joined if g == groups - 1 else 1), lanes, halves

    def x_copy(s):
        n, lanes, _ = part_of(s)
        return pltpu.make_async_remote_copy(
            src_ref=x_send.at[n, lanes], dst_ref=x_recv.at[n, lanes], send_sem=xs_sem.at[s],
            recv_sem=xr_sem.at[s], device_id=(me, other_map), device_id_type=mesh_id)

    own_slots = pl.ds(pl.multiple_of(me * cap, cap), cap)

    def produce(n):
        spectrum(last, n)
        for odd_row in range(2):
            table = cross[odd_row * rows:(odd_row + 1) * rows, :]
            y = jnp.dot(table, right[n, odd_row], preferred_element_type=f32)
            to = slice(odd_row * half_rows, (odd_row + 1) * half_rows)
            for p in range(2):
                cut = slice(p * LANES, (p + 1) * LANES)
                x_send[n, p, to, :] = y[:half_rows, cut].astype(bf16)
                x_own[n, p, to, :] = y[half_rows:, cut]
        for s in range(parts):
            if part_of(s)[0] == n:
                x_copy(s).start()

    def route(s):
        n, lanes, halves = part_of(s)
        x_copy(s).wait_recv()
        image = jnp.concatenate([
            (x_own[n, p] + x_recv[n, p].astype(f32)).astype(bf16) for p in halves], axis=1)
        slotted = jnp.dot(slot_hot[...], image, preferred_element_type=f32).astype(bf16)
        for at, p in enumerate(halves):
            packed[n, p] = slotted[:, at * LANES:(at + 1) * LANES]

        for p in halves:
            arrived[n, p, own_slots, :] = packed[n, p, own_slots, :]
        if groups - 1 <= s < parts - 1:
            return
        g = min(s, groups - 1)
        _, span_of, lanes, _ = group_of(g)

        def send(i, _):
            to = jnp.where(i - 1 < me, i - 1, i) if g == groups - 1 else lax.rem(me + i, blk)
            pltpu.make_async_remote_copy(
                src_ref=packed.at[span_of, lanes, pl.ds(pl.multiple_of(to * cap, cap), cap)],
                dst_ref=arrived.at[span_of, lanes, own_slots], send_sem=as_sem.at[g],
                recv_sem=ar_sem.at[g], device_id=(to, my_map),
                device_id_type=mesh_id).start()
            return 0

        lax.fori_loop(1, blk, send, 0)

    produce(0)
    for s in range(parts):
        n = part_of(s)[0]
        if (s == 0 or part_of(s - 1)[0] != n) and n + 1 < chunks:
            produce(n + 1)
        route(s)

    def wait_bytes(ref, sem):
        pltpu.make_async_copy(ref, ref, sem).wait()

    others = pl.ds(0, (blk - 1) * cap)

    accs = ((u_acc, 0), (v_acc, LANES))

    def product(n, at, cut):
        return jnp.dot(
            arrived[n, at // LANES, cut, :], weights[n * LANES:(n + 1) * LANES, :],
            preferred_element_type=f32)

    every = slice(0, slots)

    def interp(g):
        n, span_of, lanes, halves = group_of(g)
        wait_bytes(arrived.at[span_of, lanes, others], ar_sem.at[g])
        if g == groups - 1:
            return
        for acc, at in accs:
            if at // LANES not in halves:
                continue
            if n == 0:
                acc[...] = product(n, at, every)
            else:
                acc[...] += product(n, at, every)

    for g in range(groups - 1):
        interp(g)
    wait_bytes(o_recv.at[pl.ds(0, blk - 1)], or_sem)
    per = LANES // cap
    group = 2 * LANES if slots % (2 * LANES) == 0 else LANES
    for g in range(blk // per):
        mark = o_recv[g * per]
        for j in range(1, per):
            mark = mark + o_recv[g * per + j]
        spot = iota((MAPH, LANES), 0) == mark.astype(jnp.int32) - 1
        spots[:, g * LANES:(g + 1) * LANES] = spot.astype(f32).astype(bf16)
    interp(groups - 1)
    final = group_of(groups - 1)[3]
    late = chunks - joined
    span_out = 2 * LANES
    for c in range(0, columns, span_out):
        to = slice(c, c + span_out)
        total = jnp.zeros((MAPH, span_out), f32)
        for g in range(slots // group):
            cut = slice(g * group, (g + 1) * group)
            power = 0.0
            for acc, at in accs:
                value = acc[cut, to]
                if chunks > 1 and at // LANES in final:
                    came = jnp.concatenate(
                        [arrived[n, at // LANES, cut, :] for n in range(late, chunks)], axis=1)
                    value = value + jnp.dot(
                        came, weights[late * LANES:, to], preferred_element_type=f32)
                power = power + value * value
            high = power.astype(bf16)
            mid = (power - high.astype(f32)).astype(bf16)
            for part in (high, mid):
                total = total + jnp.dot(spots[:, cut], part, preferred_element_type=f32)
        out_ref[:, to] = total

    def sent(kind):
        for h in range(2):
            wait_bytes(half_of(0, h), g_send.at[kind, h])

    for kind in (0, 4, 5, 6):
        sent(kind)
    for kind, used in (
            (1, core == 1), (2, quad != 1), (3, quad != 3), (7, core == 0), (8, quad == 1), (9, quad == 2)):
        pl.when(used)(functools.partial(sent, kind))
    for s in range(parts):
        n, lanes, _ = part_of(s)
        wait_bytes(x_send.at[n, lanes], xs_sem.at[s])
    for g in range(groups):
        _, span_of, lanes, _ = group_of(g)
        wait_bytes(packed.at[span_of, lanes, others], as_sem.at[g])
    wait_bytes(o_send.at[pl.ds(0, blk - 1)], os_sem)


def body(phase_history, tile_curvature, interp_weights, strip_tiles, row_offsets, tile_owner):
    blk = lax.axis_size("blk")
    maps = lax.axis_size("map")
    pulses = phase_history.shape[2]
    freqs = phase_history.shape[3] // 2
    columns = interp_weights.shape[2]
    rows = strip_tiles.shape[2]
    cap = max(TILE, 2 * rows // blk)
    slots = blk * cap
    chunks = columns // LANES
    width = 2 * LANES
    stacked = STOPS // 2 * pulses
    f32, bf16 = jnp.float32, jnp.bfloat16
    hbm = pl.BlockSpec(memory_space=pltpu.HBM)
    vmem = pl.BlockSpec(memory_space=pltpu.VMEM)
    dma = pltpu.SemaphoreType.DMA
    in_hbm = functools.partial(pltpu.with_memory_space_constraint, memory_space=pltpu.HBM)
    out = pl.pallas_call(
        functools.partial(kernel, (blk, maps, pulses, freqs, columns, rows, cap)),
        out_shape=jax.ShapeDtypeStruct((MAPH, columns), f32),
        in_specs=[hbm, pl.BlockSpec(memory_space=pltpu.SMEM), hbm, hbm, hbm, hbm],
        out_specs=vmem,
        scratch_shapes=[
            pltpu.VMEM((columns, columns), bf16),
            pltpu.VMEM((1, rows), jnp.int32),
            pltpu.VMEM((1, rows), jnp.int32),
            pltpu.VMEM((1, blk), jnp.int32),
            dma((5,)),
            pltpu.VMEM((STOPS, 2, pulses, freqs), f32),
            pltpu.VMEM((STOPS, pulses, 2 * freqs), bf16),
            pltpu.VMEM((chunks, freqs, width), bf16),
            pltpu.VMEM((rows * maps, 2 * stacked), bf16),
            pltpu.VMEM((2, 2 * pulses, freqs), bf16),
            pltpu.VMEM((chunks, 2, 2 * stacked, width), bf16),
            pltpu.VMEM((columns, columns), bf16),
            pltpu.VMEM((chunks, 2, rows, LANES), bf16),
            pltpu.VMEM((chunks, 2, rows, LANES), bf16),
            pltpu.VMEM((chunks, 2, rows, LANES), f32),
            pltpu.VMEM((chunks, 2, slots, LANES), bf16),
            pltpu.VMEM((chunks, 2, slots, LANES), bf16),
            pltpu.VMEM((slots, rows), bf16),
            pltpu.VMEM((blk, 1, LANES), f32),
            pltpu.VMEM((blk, 1, LANES), f32),
            pltpu.VMEM((slots, columns), f32),
            pltpu.VMEM((slots, columns), f32),
            pltpu.VMEM((MAPH, slots), bf16),
            dma((10, 2)), dma((STOPS, 2)), dma((chunks + 1,)), dma((chunks + 1,)),
            dma((chunks + 1,)), dma((chunks + 1,)), dma, dma,
        ],
        compiler_params=pltpu.CompilerParams(
            collective_id=0, has_side_effects=True, vmem_limit_bytes=40 * 2**20),
    )(
        in_hbm(phase_history[0, 0]), tile_curvature, in_hbm(interp_weights[0]),
        in_hbm(strip_tiles[0, 0].reshape(1, rows)), in_hbm(row_offsets[0]),
        in_hbm(tile_owner.reshape(1, blk)),
    )
    return jnp.maximum(out, 0.0).reshape(1, 1, MAPH, columns)


def solution(mesh):
    in_specs = (
        P("blk", "map", None, None),
        P("blk"),
        P("blk", None, None),
        P("blk", "map", None, None),
        P("blk", "map", None),
        P(),
    )
    out_specs = P("blk", "map", None, None)
    return jax.shard_map(body, mesh=mesh, in_specs=in_specs, out_specs=out_specs, check_vma=False)
```

```python
import functools
import math

import jax
import jax.numpy as jnp
import numpy as np
from jax import lax
from jax.experimental import pallas as pl
from jax.experimental.pallas import tpu as pltpu
from jax.sharding import PartitionSpec as P

STOPS = 8
MAPH = 256
LANES = 128
TILE = 16


def fit_turns():
    z = 0.125 - 0.125 * np.cos(np.pi * (np.arange(400) + 0.5) / 400)
    t = np.sqrt(z)
    cheb = np.polynomial.chebyshev.Chebyshev
    cos_fit = cheb.fit(z, np.cos(2 * np.pi * t), 7, domain=[0, 0.25])
    sin_fit = cheb.fit(z, np.sin(2 * np.pi * t) / t, 6, domain=[0, 0.25])
    power = np.polynomial.Polynomial
    return (
        [float(np.float32(c)) for c in cos_fit.convert(kind=power).coef],
        [float(np.float32(c)) for c in sin_fit.convert(kind=power).coef],
    )


COS_COEF, SIN_COEF = fit_turns()


def cos_sin_turns(turns):
    t = turns - jnp.round(turns)
    z = t * t
    c = jnp.full_like(z, COS_COEF[-1])
    for coef in COS_COEF[-2::-1]:
        c = c * z + coef
    s = jnp.full_like(z, SIN_COEF[-1])
    for coef in SIN_COEF[-2::-1]:
        s = s * z + coef
    return c, s * t


def iota(shape, axis):
    return lax.broadcasted_iota(jnp.int32, shape, axis)


def kernel(
    sizes,
    block_hbm, curv_ref, weight_hbm, tiles_hbm, offs_hbm, owner_hbm,
    out_ref,
    weight_ref, tiles_ref, offs_ref, owner_ref, in_sem, trig, blocks, ranges, cross, phased, right, weights, x_send, x_recv, x_own, packed, arrived, slot_hot,
    o_send, o_recv, u_acc, v_acc, spots,
    g_send, g_recv, xs_sem, xr_sem, as_sem, ar_sem, os_sem, or_sem,
):
    blk, maps, pulses, freqs, columns, rows, cap = sizes
    f32, bf16 = jnp.float32, jnp.bfloat16
    me = lax.axis_index("blk")
    my_map = lax.axis_index("map")
    other_map = 1 - my_map
    core = lax.rem(me, 2)
    span = STOPS * maps * pulses
    stacked = STOPS // 2 * pulses
    chunks = columns // LANES
    width = 2 * LANES
    slots = blk * cap
    own_stop = STOPS // 2 - 1

    def device(index):
        return (lax.rem(index + 2 * blk, blk), my_map)

    mesh_id = pl.DeviceIdType.MESH

    barrier = pltpu.get_barrier_semaphore()

    def greet(i, _):
        pl.semaphore_signal(barrier, inc=1, device_id=device(me + i), device_id_type=mesh_id)
        return 0

    lax.fori_loop(1, blk, greet, 0)
    pl.semaphore_signal(barrier, inc=1, device_id=(me, other_map), device_id_type=mesh_id)

    def bring(source, target, sem):
        return pltpu.make_async_copy(source, target, in_sem.at[sem])

    inputs = [
        bring(block_hbm, blocks.at[own_stop], 0),
        bring(owner_hbm, owner_ref, 1),
        bring(tiles_hbm, tiles_ref, 2),
        bring(offs_hbm, offs_ref, 3),
        bring(weight_hbm, weight_ref, 4),
    ]
    for copy in inputs:
        copy.start()
    inputs[0].wait()
    pl.semaphore_wait(barrier, blk)

    partner = device(me + 1 - 2 * core)
    shift = 2 * core - 1
    quad = lax.rem(me, 4)
    half = pulses // 2
    last = 2 - core

    def half_of(stop, h):
        return blocks.at[stop, pl.ds(h * half, half)]

    def push(source, stop, h, target, kind):
        pltpu.make_async_remote_copy(
            src_ref=half_of(source, h), dst_ref=half_of(stop, h), send_sem=g_send.at[kind, h],
            recv_sem=g_recv.at[stop, h], device_id=target, device_id_type=mesh_id).start()

    def push_own(stop, target, kind):
        for h in range(2):
            push(own_stop, stop, h, target, kind)

    def arrived_half(stop, h):
        pltpu.make_async_copy(half_of(stop, h), half_of(stop, h), g_recv.at[stop, h]).wait()

    def arrived_block(stop):
        for h in range(2):
            arrived_half(stop, h)

    def pass_on(stop, to_stop, target, kind):
        for h in range(2):
            arrived_half(stop, h)
            push(stop, to_stop, h, target, kind)

    @pl.when(quad == 3)
    def _():
        push_own(0, device(me + 3), 1)

    push_own(7, device(me - 4), 0)

    @pl.when(quad == 1)
    def _():
        push_own(0, device(me + 3), 1)

    @pl.when(quad != 1)
    def _():
        push_own(5, device(me - 2), 2)

    @pl.when(quad != 3)
    def _():
        push_own(1, device(me + 2), 3)

    push_own(own_stop + shift, partner, 4)

    half_freqs = freqs // 2
    half_chunks = chunks // 2
    half_rows = rows // 2

    def fill_ranges(i, _):
        at = pl.ds(pl.multiple_of(i * TILE, TILE), TILE)
        below = pl.ds(pl.multiple_of(half_freqs + i * TILE, TILE), TILE)
        f = (i * TILE + iota((TILE, columns // 2), 0)).astype(f32)
        for odd in range(2):
            c = (2 * iota((TILE, columns // 2), 1) + odd).astype(f32)
            re, im = cos_sin_turns(f * c * (1.0 / freqs))
            re = (re * (1.0 / math.sqrt(freqs))).astype(bf16)
            im = (im * (1.0 / math.sqrt(freqs)))
            pos, neg = im.astype(bf16), (-im).astype(bf16)
            for n in range(half_chunks):
                cut = slice(n * LANES, (n + 1) * LANES)
                to = odd * half_chunks + n
                ranges[to, at, 0:LANES] = re[:, cut]
                ranges[to, at, LANES:width] = neg[:, cut]
                ranges[to, below, 0:LANES] = pos[:, cut]
                ranges[to, below, LANES:width] = re[:, cut]
        return 0

    lax.fori_loop(0, half_freqs // TILE, fill_ranges, 0)

    lane = iota((1, stacked), 1)
    q_lane = (lane + (lax.div(lane, pulses) * (maps - 1) + my_map) * pulses).astype(f32)

    def fill_cross(i, _):
        at = pl.ds(pl.multiple_of(i * TILE, TILE), TILE)
        g = i * TILE
        odd = lax.div(g, rows)
        own = lax.div(lax.rem(g, rows), half_rows)
        part = jnp.where(own == 1, my_map, other_map)
        base = part * rows + odd + 2 * lax.rem(g, half_rows)
        a = (base + 2 * iota((TILE, stacked), 0)).astype(f32)
        re, im = cos_sin_turns(a * q_lane * (1.0 / span))
        cross[at, 0:stacked] = (re * (1.0 / math.sqrt(span))).astype(bf16)
        cross[at, stacked:2 * stacked] = (im * (-1.0 / math.sqrt(span))).astype(bf16)
        return 0

    lax.fori_loop(0, rows * maps // TILE, fill_cross, 0)

    def fill_slots():
        tiles = tiles_ref[...]
        holders = iota((blk, rows), 0)
        named = (holders == tiles).astype(f32).astype(bf16)
        holds = (iota((blk, blk), 0) == owner_ref[...]).astype(f32).astype(bf16)
        hot = jnp.dot(holds, named, preferred_element_type=f32)
        dest = jnp.sum(holders.astype(f32) * hot, axis=0, keepdims=True).astype(jnp.int32)
        upto = (iota((rows, rows), 0) <= iota((rows, rows), 1)).astype(f32).astype(bf16)
        counts = jnp.dot(hot.astype(bf16), upto, preferred_element_type=f32)
        rank = jnp.sum(counts * hot, axis=0, keepdims=True).astype(jnp.int32) - 1
        slot = dest * cap + rank
        spot = iota((rows, rows), 1)
        spot = 2 * lax.rem(spot, half_rows) + lax.div(spot, half_rows)
        order = (iota((rows, rows), 0) == spot).astype(f32).astype(bf16)
        for i in range(slots // LANES):
            at = i * LANES + iota((LANES, rows), 0)
            hits = (at == slot).astype(f32).astype(bf16)
            slot_hot[i * LANES:(i + 1) * LANES, :] = jnp.dot(
                hits, order, preferred_element_type=f32).astype(bf16)
        place = lax.rem(me, LANES // cap) * cap + rank
        marks = jnp.where(iota((LANES, rows), 0) == place, (offs_ref[...] + 1).astype(f32), 0.0)
        table = lax.dot_general(
            hot.astype(bf16), marks.astype(bf16), (((1,), (1,)), ((), ())),
            preferred_element_type=f32)
        for d in range(blk):
            o_send[d] = table[d:d + 1, :]
        o_recv[me] = o_send[me]

        def send(i, _):
            to = lax.rem(me + i, blk)
            pltpu.make_async_remote_copy(
                src_ref=o_send.at[to], dst_ref=o_recv.at[me], send_sem=os_sem,
                recv_sem=or_sem, device_id=(to, my_map), device_id_type=mesh_id).start()
            return 0

        lax.fori_loop(1, blk, send, 0)

    for copy in inputs[1:]:
        copy.wait()
    fill_slots()

    def order_weights(i, _):
        at = pl.ds(pl.multiple_of(i * LANES, LANES), LANES)
        r = i * LANES + iota((LANES, columns), 0)
        r = 2 * lax.rem(r, columns // 2) + lax.div(r, columns // 2)
        order = (iota((LANES, columns), 1) == r).astype(f32).astype(bf16)
        weights[at, :] = jnp.dot(
            order, weight_ref[...], preferred_element_type=f32).astype(bf16)
        return 0

    lax.fori_loop(0, chunks, order_weights, 0)

    def fill_trig(i, _):
        at = pl.ds(pl.multiple_of(lax.rem(i, pulses // TILE) * TILE, TILE), TILE)
        k = lax.div(i, pulses // TILE)
        q = (k * maps + my_map) * pulses + lax.rem(i, pulses // TILE) * TILE + iota((TILE, 1), 0)
        s = q.astype(f32) * (1.0 / span) - 0.5
        r = iota((TILE, freqs), 1).astype(f32) * (1.0 / freqs) - 0.5
        angle = curv_ref[0] * (s * s) * (1.0 + r)
        c, si = cos_sin_turns(angle * (0.5 / math.pi))
        trig[k, 0, at, :] = c
        trig[k, 1, at, :] = si
        return 0

    lax.fori_loop(0, STOPS * pulses // TILE, fill_trig, 0)

    def turned(k, i):
        at = pl.ds(pl.multiple_of(i * TILE, TILE), TILE)
        c, si = trig[k, 0, at, :], trig[k, 1, at, :]
        re = blocks[k, at, 0:freqs].astype(f32)
        im = blocks[k, at, freqs:2 * freqs].astype(f32)
        return re * c - im * si, re * si + im * c

    def phase(j):
        def turn(i, _):
            first = turned(j, i)
            second = turned(j + STOPS // 2, i)
            for part in range(2):
                z_sum, z_diff = first[part] + second[part], first[part] - second[part]
                to = slice(part * half_freqs, (part + 1) * half_freqs)
                for odd_row, z in ((0, z_sum), (1, z_diff)):
                    at = pl.ds(pl.multiple_of(odd_row * pulses + i * TILE, TILE), TILE)
                    near, far = z[:, :half_freqs], z[:, half_freqs:]
                    phased[0, at, to] = (near + far).astype(bf16)
                    phased[1, at, to] = (near - far).astype(bf16)
            return 0

        lax.fori_loop(0, pulses // TILE, turn, 0, unroll=2)

    def spectrum(j, n):
        top = pl.ds(pl.multiple_of(j * pulses, pulses), pulses)
        low = pl.ds(pl.multiple_of(stacked + j * pulses, pulses), pulses)
        odd = lax.div(n, half_chunks)
        y = jnp.dot(phased[odd], ranges[n], preferred_element_type=f32)
        yr, yi = y[:, :LANES], y[:, LANES:]
        for odd_row in range(2):
            cut = slice(odd_row * pulses, (odd_row + 1) * pulses)
            real, imag = yr[cut].astype(bf16), yi[cut].astype(bf16)
            right[n, odd_row, top, 0:LANES] = real
            right[n, odd_row, top, LANES:width] = imag
            right[n, odd_row, low, 0:LANES] = (-yi[cut]).astype(bf16)
            right[n, odd_row, low, LANES:width] = real

    def near(stop):
        pass_on(stop, stop + shift, partner, jnp.where(stop == 5, 5, 6))

    near_stop = jnp.where(quad < 2, 5, 1)

    def step(i, _):
        j = jnp.where(i == 0, 3, jnp.where(i == 1, 2 * core, 1 - core))

        @pl.when(i == 0)
        def _():
            near(near_stop)

            @pl.when(quad == 1)
            def _():
                pass_on(7, 5, device(me + 2), 8)

            @pl.when(quad == 2)
            def _():
                pass_on(0, 1, device(me - 1), 9)

            @pl.when(core == 0)
            def _():
                pass_on(7, 6, partner, 7)

            @pl.when(quad == 3)
            def _():
                arrived_block(7)

        @pl.when(i == 1 + core)
        def _():
            near(6 - near_stop)

        @pl.when((j == 0) & (quad != 2))
        def _():
            arrived_block(0)

        @pl.when((j == 0) | (j == 2))
        def _():
            arrived_block(jnp.maximum(j, 0) + STOPS // 2)

        @pl.when(j == 2)
        def _():
            arrived_block(2)

        phase(j)
        for n in range(chunks):
            spectrum(j, n)
        return 0

    lax.fori_loop(0, STOPS // 2 - 1, step, 0)

    @pl.when(core == 0)
    def _():
        arrived_block(2)
        arrived_block(6)

    phase(last)
    first_parts = 2
    parts = chunks + first_parts - 1

    def part_of(s):
        if s < first_parts:
            return 0, pl.ds(s, 1), (s,)
        return s - first_parts + 1, pl.ds(0, 2), (0, 1)

    joined = 2 if chunks >= 4 else 1
    groups = parts - joined + 1

    def group_of(g):
        n, lanes, halves = part_of(g)
        return n, pl.ds(n, joined if g == groups - 1 else 1), lanes, halves

    def x_copy(s):
        n, lanes, _ = part_of(s)
        return pltpu.make_async_remote_copy(
            src_ref=x_send.at[n, lanes], dst_ref=x_recv.at[n, lanes], send_sem=xs_sem.at[s],
            recv_sem=xr_sem.at[s], device_id=(me, other_map), device_id_type=mesh_id)

    side = lax.div(me, blk // 2)
    own_slots = pl.ds(pl.multiple_of(me * cap, cap), cap)

    def produce(n):
        spectrum(last, n)
        for odd_row in range(2):
            table = cross[odd_row * rows:(odd_row + 1) * rows, :]
            y = jnp.dot(table, right[n, odd_row], preferred_element_type=f32)
            to = slice(odd_row * half_rows, (odd_row + 1) * half_rows)
            for p in range(2):
                cut = slice(p * LANES, (p + 1) * LANES)
                x_send[n, p, to, :] = y[:half_rows, cut].astype(bf16)
                x_own[n, p, to, :] = y[half_rows:, cut]
        for s in range(parts):
            if part_of(s)[0] == n:
                x_copy(s).start()

    def route(s):
        n, lanes, halves = part_of(s)
        x_copy(s).wait_recv()
        image = jnp.concatenate([
            (x_own[n, p] + x_recv[n, p].astype(f32)).astype(bf16) for p in halves], axis=1)
        slotted = jnp.dot(slot_hot[...], image, preferred_element_type=f32).astype(bf16)
        for at, p in enumerate(halves):
            packed[n, p] = slotted[:, at * LANES:(at + 1) * LANES]

        for p in halves:
            arrived[n, p, own_slots, :] = packed[n, p, own_slots, :]
        if groups - 1 <= s < parts - 1:
            return
        g = min(s, groups - 1)
        _, span_of, lanes, _ = group_of(g)

        def send(i, _):
            to = jnp.where(i - 1 < me, i - 1, i) if g == groups - 1 else lax.rem(me + i, blk)
            pltpu.make_async_remote_copy(
                src_ref=packed.at[span_of, lanes, pl.ds(pl.multiple_of(to * cap, cap), cap)],
                dst_ref=arrived.at[span_of, lanes, own_slots], send_sem=as_sem.at[g],
                recv_sem=ar_sem.at[g + (side if g == groups - 1 else 0)], device_id=(to, my_map),
                device_id_type=mesh_id).start()
            return 0

        lax.fori_loop(1, blk, send, 0)

    produce(0)
    for s in range(parts):
        n = part_of(s)[0]
        if (s == 0 or part_of(s - 1)[0] != n) and n + 1 < chunks:
            produce(n + 1)
        route(s)

    def wait_bytes(ref, sem):
        pltpu.make_async_copy(ref, ref, sem).wait()

    others = pl.ds(0, (blk - 1) * cap)

    accs = ((u_acc, 0), (v_acc, LANES))

    def product(n, at, cut):
        return jnp.dot(
            arrived[n, at // LANES, cut, :], weights[n * LANES:(n + 1) * LANES, :],
            preferred_element_type=f32)

    every = slice(0, slots)

    def interp(g):
        n, span_of, lanes, halves = group_of(g)
        wait_bytes(arrived.at[span_of, lanes, others], ar_sem.at[g])
        for acc, at in accs:
            if at // LANES not in halves:
                continue
            if n == 0:
                acc[...] = product(n, at, every)
            else:
                acc[...] += product(n, at, every)

    for g in range(groups - 1):
        interp(g)
    wait_bytes(o_recv.at[pl.ds(0, blk - 1)], or_sem)
    per = LANES // cap
    group = 2 * LANES if slots % (2 * LANES) == 0 else LANES
    for g in range(blk // per):
        mark = o_recv[g * per]
        for j in range(1, per):
            mark = mark + o_recv[g * per + j]
        spot = iota((MAPH, LANES), 0) == mark.astype(jnp.int32) - 1
        spots[:, g * LANES:(g + 1) * LANES] = spot.astype(f32).astype(bf16)
    _, span_of, lanes, final = group_of(groups - 1)
    late = chunks - joined
    span_out = 2 * LANES

    def finish(turn):
        here = side if turn == 0 else 1 - side
        came_from = pl.ds(0, (blk // 2 - 1 + turn) * cap)
        wait_bytes(arrived.at[span_of, lanes, came_from], ar_sem.at[groups - 1 + here])
        for c in range(0, columns, span_out):
            to = slice(c, c + span_out)
            total = jnp.zeros((MAPH, span_out), f32)
            for g in range(slots // 2 // group):
                cut = pl.ds(pl.multiple_of(here * (slots // 2) + g * group, group), group)
                power = 0.0
                for acc, at in accs:
                    value = acc[cut, to]
                    if chunks > 1 and at // LANES in final:
                        came = jnp.concatenate(
                            [arrived[n, at // LANES, cut, :] for n in range(late, chunks)], axis=1)
                        value = value + jnp.dot(
                            came, weights[late * LANES:, to], preferred_element_type=f32)
                    power = power + value * value
                high = power.astype(bf16)
                mid = (power - high.astype(f32)).astype(bf16)
                for part in (high, mid):
                    total = total + jnp.dot(spots[:, cut], part, preferred_element_type=f32)
            if turn == 0:
                out_ref[:, to] = total
            else:
                out_ref[:, to] += total

    finish(0)
    finish(1)

    def sent(kind):
        for h in range(2):
            wait_bytes(half_of(0, h), g_send.at[kind, h])

    for kind in (0, 4, 5, 6):
        sent(kind)
    for kind, used in (
            (1, core == 1), (2, quad != 1), (3, quad != 3), (7, core == 0), (8, quad == 1), (9, quad == 2)):
        pl.when(used)(functools.partial(sent, kind))
    for s in range(parts):
        n, lanes, _ = part_of(s)
        wait_bytes(x_send.at[n, lanes], xs_sem.at[s])
    for g in range(groups):
        _, span_of, lanes, _ = group_of(g)
        wait_bytes(packed.at[span_of, lanes, others], as_sem.at[g])
    wait_bytes(o_send.at[pl.ds(0, blk - 1)], os_sem)


def body(phase_history, tile_curvature, interp_weights, strip_tiles, row_offsets, tile_owner):
    blk = lax.axis_size("blk")
    maps = lax.axis_size("map")
    pulses = phase_history.shape[2]
    freqs = phase_history.shape[3] // 2
    columns = interp_weights.shape[2]
    rows = strip_tiles.shape[2]
    cap = max(TILE, 2 * rows // blk)
    slots = blk * cap
    chunks = columns // LANES
    width = 2 * LANES
    stacked = STOPS // 2 * pulses
    f32, bf16 = jnp.float32, jnp.bfloat16
    hbm = pl.BlockSpec(memory_space=pltpu.HBM)
    vmem = pl.BlockSpec(memory_space=pltpu.VMEM)
    dma = pltpu.SemaphoreType.DMA
    in_hbm = functools.partial(pltpu.with_memory_space_constraint, memory_space=pltpu.HBM)
    out = pl.pallas_call(
        functools.partial(kernel, (blk, maps, pulses, freqs, columns, rows, cap)),
        out_shape=jax.ShapeDtypeStruct((MAPH, columns), f32),
        in_specs=[hbm, pl.BlockSpec(memory_space=pltpu.SMEM), hbm, hbm, hbm, hbm],
        out_specs=vmem,
        scratch_shapes=[
            pltpu.VMEM((columns, columns), bf16),
            pltpu.VMEM((1, rows), jnp.int32),
            pltpu.VMEM((1, rows), jnp.int32),
            pltpu.VMEM((1, blk), jnp.int32),
            dma((5,)),
            pltpu.VMEM((STOPS, 2, pulses, freqs), f32),
            pltpu.VMEM((STOPS, pulses, 2 * freqs), bf16),
            pltpu.VMEM((chunks, freqs, width), bf16),
            pltpu.VMEM((rows * maps, 2 * stacked), bf16),
            pltpu.VMEM((2, 2 * pulses, freqs), bf16),
            pltpu.VMEM((chunks, 2, 2 * stacked, width), bf16),
            pltpu.VMEM((columns, columns), bf16),
            pltpu.VMEM((chunks, 2, rows, LANES), bf16),
            pltpu.VMEM((chunks, 2, rows, LANES), bf16),
            pltpu.VMEM((chunks, 2, rows, LANES), f32),
            pltpu.VMEM((chunks, 2, slots, LANES), bf16),
            pltpu.VMEM((chunks, 2, slots, LANES), bf16),
            pltpu.VMEM((slots, rows), bf16),
            pltpu.VMEM((blk, 1, LANES), f32),
            pltpu.VMEM((blk, 1, LANES), f32),
            pltpu.VMEM((slots, columns), f32),
            pltpu.VMEM((slots, columns), f32),
            pltpu.VMEM((MAPH, slots), bf16),
            dma((10, 2)), dma((STOPS, 2)), dma((chunks + 1,)), dma((chunks + 1,)),
            dma((chunks + 1,)), dma((chunks + 2,)), dma, dma,
        ],
        compiler_params=pltpu.CompilerParams(
            collective_id=0, has_side_effects=True, vmem_limit_bytes=40 * 2**20),
    )(
        in_hbm(phase_history[0, 0]), tile_curvature, in_hbm(interp_weights[0]),
        in_hbm(strip_tiles[0, 0].reshape(1, rows)), in_hbm(row_offsets[0]),
        in_hbm(tile_owner.reshape(1, blk)),
    )
    return jnp.maximum(out, 0.0).reshape(1, 1, MAPH, columns)


def solution(mesh):
    in_specs = (
        P("blk", "map", None, None),
        P("blk"),
        P("blk", None, None),
        P("blk", "map", None, None),
        P("blk", "map", None),
        P(),
    )
    out_specs = P("blk", "map", None, None)
    return jax.shard_map(body, mesh=mesh, in_specs=in_specs, out_specs=out_specs, check_vma=False)
```

```python
import functools
import math

import jax
import jax.numpy as jnp
import numpy as np
from jax import lax
from jax.experimental import pallas as pl
from jax.experimental.pallas import tpu as pltpu
from jax.sharding import PartitionSpec as P

STOPS = 8
MAPH = 256
LANES = 128
TILE = 16


def fit_turns():
    z = 0.125 - 0.125 * np.cos(np.pi * (np.arange(400) + 0.5) / 400)
    t = np.sqrt(z)
    cheb = np.polynomial.chebyshev.Chebyshev
    cos_fit = cheb.fit(z, np.cos(2 * np.pi * t), 7, domain=[0, 0.25])
    sin_fit = cheb.fit(z, np.sin(2 * np.pi * t) / t, 6, domain=[0, 0.25])
    power = np.polynomial.Polynomial
    return (
        [float(np.float32(c)) for c in cos_fit.convert(kind=power).coef],
        [float(np.float32(c)) for c in sin_fit.convert(kind=power).coef],
    )


COS_COEF, SIN_COEF = fit_turns()


def cos_sin_turns(turns):
    t = turns - jnp.round(turns)
    z = t * t
    c = jnp.full_like(z, COS_COEF[-1])
    for coef in COS_COEF[-2::-1]:
        c = c * z + coef
    s = jnp.full_like(z, SIN_COEF[-1])
    for coef in SIN_COEF[-2::-1]:
        s = s * z + coef
    return c, s * t


def iota(shape, axis):
    return lax.broadcasted_iota(jnp.int32, shape, axis)


def kernel(
    sizes,
    block_hbm, curv_ref, weight_hbm, tiles_hbm, offs_hbm, owner_hbm,
    out_ref,
    weight_ref, tiles_ref, offs_ref, owner_ref, in_sem, trig, blocks, ranges, cross, phased, right, weights, x_send, x_recv, x_own, packed, arrived, slot_hot,
    o_send, o_recv, u_acc, v_acc, spots,
    g_send, g_recv, xs_sem, xr_sem, as_sem, ar_sem, os_sem, or_sem,
):
    blk, maps, pulses, freqs, columns, rows, cap = sizes
    f32, bf16 = jnp.float32, jnp.bfloat16
    me = lax.axis_index("blk")
    my_map = lax.axis_index("map")
    other_map = 1 - my_map
    core = lax.rem(me, 2)
    span = STOPS * maps * pulses
    stacked = STOPS // 2 * pulses
    chunks = columns // LANES
    width = 2 * LANES
    slots = blk * cap
    own_stop = STOPS // 2 - 1

    def device(index):
        return (lax.rem(index + 2 * blk, blk), my_map)

    mesh_id = pl.DeviceIdType.MESH

    barrier = pltpu.get_barrier_semaphore()

    def greet(i, _):
        pl.semaphore_signal(barrier, inc=1, device_id=device(me + i), device_id_type=mesh_id)
        return 0

    lax.fori_loop(1, blk, greet, 0)
    pl.semaphore_signal(barrier, inc=1, device_id=(me, other_map), device_id_type=mesh_id)

    def bring(source, target, sem):
        return pltpu.make_async_copy(source, target, in_sem.at[sem])

    inputs = [
        bring(block_hbm, blocks.at[own_stop], 0),
        bring(owner_hbm, owner_ref, 1),
        bring(tiles_hbm, tiles_ref, 2),
        bring(offs_hbm, offs_ref, 3),
        bring(weight_hbm, weight_ref, 4),
    ]
    for copy in inputs:
        copy.start()
    inputs[0].wait()
    pl.semaphore_wait(barrier, blk)

    partner = device(me + 1 - 2 * core)
    shift = 2 * core - 1
    quad = lax.rem(me, 4)
    half = pulses // 2
    last = 2 - core

    def half_of(stop, h):
        return blocks.at[stop, pl.ds(h * half, half)]

    def push(source, stop, h, target, kind):
        pltpu.make_async_remote_copy(
            src_ref=half_of(source, h), dst_ref=half_of(stop, h), send_sem=g_send.at[kind, h],
            recv_sem=g_recv.at[stop, h], device_id=target, device_id_type=mesh_id).start()

    def push_own(stop, target, kind):
        for h in range(2):
            push(own_stop, stop, h, target, kind)

    def arrived_half(stop, h):
        pltpu.make_async_copy(half_of(stop, h), half_of(stop, h), g_recv.at[stop, h]).wait()

    def arrived_block(stop):
        for h in range(2):
            arrived_half(stop, h)

    def pass_on(stop, to_stop, target, kind):
        for h in range(2):
            arrived_half(stop, h)
            push(stop, to_stop, h, target, kind)

    @pl.when(quad == 3)
    def _():
        push_own(0, device(me + 3), 1)

    push_own(7, device(me - 4), 0)

    @pl.when(quad == 1)
    def _():
        push_own(0, device(me + 3), 1)

    @pl.when(quad != 1)
    def _():
        push_own(5, device(me - 2), 2)

    @pl.when(quad != 3)
    def _():
        push_own(1, device(me + 2), 3)

    push_own(own_stop + shift, partner, 4)

    half_freqs = freqs // 2
    half_chunks = chunks // 2
    half_rows = rows // 2

    def fill_ranges(i, _):
        at = pl.ds(pl.multiple_of(i * TILE, TILE), TILE)
        below = pl.ds(pl.multiple_of(half_freqs + i * TILE, TILE), TILE)
        f = (i * TILE + iota((TILE, columns // 2), 0)).astype(f32)
        for odd in range(2):
            c = (2 * iota((TILE, columns // 2), 1) + odd).astype(f32)
            re, im = cos_sin_turns(f * c * (1.0 / freqs))
            re = (re * (1.0 / math.sqrt(freqs))).astype(bf16)
            im = (im * (1.0 / math.sqrt(freqs)))
            pos, neg = im.astype(bf16), (-im).astype(bf16)
            for n in range(half_chunks):
                cut = slice(n * LANES, (n + 1) * LANES)
                to = odd * half_chunks + n
                ranges[to, at, 0:LANES] = re[:, cut]
                ranges[to, at, LANES:width] = neg[:, cut]
                ranges[to, below, 0:LANES] = pos[:, cut]
                ranges[to, below, LANES:width] = re[:, cut]
        return 0

    lax.fori_loop(0, half_freqs // TILE, fill_ranges, 0)

    lane = iota((1, stacked), 1)
    q_lane = (lane + (lax.div(lane, pulses) * (maps - 1) + my_map) * pulses).astype(f32)

    def fill_cross(i, _):
        at = pl.ds(pl.multiple_of(i * TILE, TILE), TILE)
        g = i * TILE
        odd = lax.div(g, rows)
        own = lax.div(lax.rem(g, rows), half_rows)
        part = jnp.where(own == 1, my_map, other_map)
        base = part * rows + odd + 2 * lax.rem(g, half_rows)
        a = (base + 2 * iota((TILE, stacked), 0)).astype(f32)
        re, im = cos_sin_turns(a * q_lane * (1.0 / span))
        cross[at, 0:stacked] = (re * (1.0 / math.sqrt(span))).astype(bf16)
        cross[at, stacked:2 * stacked] = (im * (-1.0 / math.sqrt(span))).astype(bf16)
        return 0

    lax.fori_loop(0, rows * maps // TILE, fill_cross, 0)

    def fill_slots():
        tiles = tiles_ref[...]
        holders = iota((blk, rows), 0)
        named = (holders == tiles).astype(f32).astype(bf16)
        holds = (iota((blk, blk), 0) == owner_ref[...]).astype(f32).astype(bf16)
        hot = jnp.dot(holds, named, preferred_element_type=f32)
        dest = jnp.sum(holders.astype(f32) * hot, axis=0, keepdims=True).astype(jnp.int32)
        upto = (iota((rows, rows), 0) <= iota((rows, rows), 1)).astype(f32).astype(bf16)
        counts = jnp.dot(hot.astype(bf16), upto, preferred_element_type=f32)
        rank = jnp.sum(counts * hot, axis=0, keepdims=True).astype(jnp.int32) - 1
        slot = dest * cap + rank
        spot = iota((rows, rows), 1)
        spot = 2 * lax.rem(spot, half_rows) + lax.div(spot, half_rows)
        order = (iota((rows, rows), 0) == spot).astype(f32).astype(bf16)
        for i in range(slots // LANES):
            at = i * LANES + iota((LANES, rows), 0)
            hits = (at == slot).astype(f32).astype(bf16)
            slot_hot[i * LANES:(i + 1) * LANES, :] = jnp.dot(
                hits, order, preferred_element_type=f32).astype(bf16)
        place = lax.rem(me, LANES // cap) * cap + rank
        marks = jnp.where(iota((LANES, rows), 0) == place, (offs_ref[...] + 1).astype(f32), 0.0)
        table = lax.dot_general(
            hot.astype(bf16), marks.astype(bf16), (((1,), (1,)), ((), ())),
            preferred_element_type=f32)
        for d in range(blk):
            o_send[d] = table[d:d + 1, :]
        o_recv[me] = o_send[me]

        def send(i, _):
            to = lax.rem(me + i, blk)
            pltpu.make_async_remote_copy(
                src_ref=o_send.at[to], dst_ref=o_recv.at[me], send_sem=os_sem,
                recv_sem=or_sem, device_id=(to, my_map), device_id_type=mesh_id).start()
            return 0

        lax.fori_loop(1, blk, send, 0)

    for copy in inputs[1:]:
        copy.wait()
    fill_slots()

    def order_weights(i, _):
        at = pl.ds(pl.multiple_of(i * LANES, LANES), LANES)
        r = i * LANES + iota((LANES, columns), 0)
        r = 2 * lax.rem(r, columns // 2) + lax.div(r, columns // 2)
        order = (iota((LANES, columns), 1) == r).astype(f32).astype(bf16)
        weights[at, :] = jnp.dot(
            order, weight_ref[...], preferred_element_type=f32).astype(bf16)
        return 0

    lax.fori_loop(0, chunks, order_weights, 0)

    def fill_trig(i, _):
        at = pl.ds(pl.multiple_of(lax.rem(i, pulses // TILE) * TILE, TILE), TILE)
        k = lax.div(i, pulses // TILE)
        q = (k * maps + my_map) * pulses + lax.rem(i, pulses // TILE) * TILE + iota((TILE, 1), 0)
        s = q.astype(f32) * (1.0 / span) - 0.5
        r = iota((TILE, freqs), 1).astype(f32) * (1.0 / freqs) - 0.5
        angle = curv_ref[0] * (s * s) * (1.0 + r)
        c, si = cos_sin_turns(angle * (0.5 / math.pi))
        trig[k, 0, at, :] = c
        trig[k, 1, at, :] = si
        return 0

    lax.fori_loop(0, STOPS * pulses // TILE, fill_trig, 0)

    def turned(k, i):
        at = pl.ds(pl.multiple_of(i * TILE, TILE), TILE)
        c, si = trig[k, 0, at, :], trig[k, 1, at, :]
        re = blocks[k, at, 0:freqs].astype(f32)
        im = blocks[k, at, freqs:2 * freqs].astype(f32)
        return re * c - im * si, re * si + im * c

    def phase(j):
        def turn(i, _):
            first = turned(j, i)
            second = turned(j + STOPS // 2, i)
            for part in range(2):
                z_sum, z_diff = first[part] + second[part], first[part] - second[part]
                to = slice(part * half_freqs, (part + 1) * half_freqs)
                for odd_row, z in ((0, z_sum), (1, z_diff)):
                    at = pl.ds(pl.multiple_of(odd_row * pulses + i * TILE, TILE), TILE)
                    near, far = z[:, :half_freqs], z[:, half_freqs:]
                    phased[0, at, to] = (near + far).astype(bf16)
                    phased[1, at, to] = (near - far).astype(bf16)
            return 0

        lax.fori_loop(0, pulses // TILE, turn, 0, unroll=2)

    def spectrum(j, n):
        top = pl.ds(pl.multiple_of(j * pulses, pulses), pulses)
        low = pl.ds(pl.multiple_of(stacked + j * pulses, pulses), pulses)
        odd = lax.div(n, half_chunks)
        y = jnp.dot(phased[odd], ranges[n], preferred_element_type=f32)
        yr, yi = y[:, :LANES], y[:, LANES:]
        for odd_row in range(2):
            cut = slice(odd_row * pulses, (odd_row + 1) * pulses)
            real, imag = yr[cut].astype(bf16), yi[cut].astype(bf16)
            right[n, odd_row, top, 0:LANES] = real
            right[n, odd_row, top, LANES:width] = imag
            right[n, odd_row, low, 0:LANES] = (-yi[cut]).astype(bf16)
            right[n, odd_row, low, LANES:width] = real

    def near(stop):
        pass_on(stop, stop + shift, partner, jnp.where(stop == 5, 5, 6))

    near_stop = jnp.where(quad < 2, 5, 1)

    def step(i, _):
        j = jnp.where(i == 0, 3, jnp.where(i == 1, 2 * core, 1 - core))

        @pl.when(i == 0)
        def _():
            near(near_stop)

            @pl.when(quad == 1)
            def _():
                pass_on(7, 5, device(me + 2), 8)

            @pl.when(quad == 2)
            def _():
                pass_on(0, 1, device(me - 1), 9)

            @pl.when(core == 0)
            def _():
                pass_on(7, 6, partner, 7)

            @pl.when(quad == 3)
            def _():
                arrived_block(7)

        @pl.when(i == 1 + core)
        def _():
            near(6 - near_stop)

        @pl.when((j == 0) & (quad != 2))
        def _():
            arrived_block(0)

        @pl.when((j == 0) | (j == 2))
        def _():
            arrived_block(jnp.maximum(j, 0) + STOPS // 2)

        @pl.when(j == 2)
        def _():
            arrived_block(2)

        phase(j)
        for n in range(chunks):
            spectrum(j, n)
        return 0

    lax.fori_loop(0, STOPS // 2 - 1, step, 0)

    @pl.when(core == 0)
    def _():
        arrived_block(2)
        arrived_block(6)

    phase(last)
    first_parts = 2
    parts = chunks + first_parts - 1

    def part_of(s):
        if s < first_parts:
            return 0, pl.ds(s, 1), (s,)
        return s - first_parts + 1, pl.ds(0, 2), (0, 1)

    joined = 2 if chunks >= 4 else 1
    groups = parts - joined + 1

    def group_of(g):
        n, lanes, halves = part_of(g)
        return n, pl.ds(n, joined if g == groups - 1 else 1), lanes, halves

    def x_copy(s):
        n, lanes, _ = part_of(s)
        return pltpu.make_async_remote_copy(
            src_ref=x_send.at[n, lanes], dst_ref=x_recv.at[n, lanes], send_sem=xs_sem.at[s],
            recv_sem=xr_sem.at[s], device_id=(me, other_map), device_id_type=mesh_id)

    side = lax.div(me, blk // 2)
    own_slots = pl.ds(pl.multiple_of(me * cap, cap), cap)

    def produce(n):
        spectrum(last, n)
        for odd_row in range(2):
            table = cross[odd_row * rows:(odd_row + 1) * rows, :]
            y = jnp.dot(table, right[n, odd_row], preferred_element_type=f32)
            to = slice(odd_row * half_rows, (odd_row + 1) * half_rows)
            for p in range(2):
                cut = slice(p * LANES, (p + 1) * LANES)
                x_send[n, p, to, :] = y[:half_rows, cut].astype(bf16)
                x_own[n, p, to, :] = y[half_rows:, cut]
        for s in range(parts):
            if part_of(s)[0] == n:
                x_copy(s).start()

    def route(s):
        n, lanes, halves = part_of(s)
        x_copy(s).wait_recv()
        image = jnp.concatenate([
            (x_own[n, p] + x_recv[n, p].astype(f32)).astype(bf16) for p in halves], axis=1)
        slotted = jnp.dot(slot_hot[...], image, preferred_element_type=f32).astype(bf16)
        for at, p in enumerate(halves):
            packed[n, p] = slotted[:, at * LANES:(at + 1) * LANES]

        for p in halves:
            arrived[n, p, own_slots, :] = packed[n, p, own_slots, :]
        if groups - 1 <= s < parts - 1:
            return
        g = min(s, groups - 1)
        _, span_of, lanes, _ = group_of(g)

        def send(i, _):
            to = jnp.where(i - 1 < me, i - 1, i) if g == groups - 1 else lax.rem(me + i, blk)
            pltpu.make_async_remote_copy(
                src_ref=packed.at[span_of, lanes, pl.ds(pl.multiple_of(to * cap, cap), cap)],
                dst_ref=arrived.at[span_of, lanes, own_slots], send_sem=as_sem.at[g],
                recv_sem=ar_sem.at[g + (side if g == groups - 1 else 0)], device_id=(to, my_map),
                device_id_type=mesh_id).start()
            return 0

        lax.fori_loop(1, blk, send, 0, unroll=3)

    produce(0)
    for s in range(parts):
        if s + 1 < chunks:
            produce(s + 1)
        route(s)

    def wait_bytes(ref, sem):
        pltpu.make_async_copy(ref, ref, sem).wait()

    others = pl.ds(0, (blk - 1) * cap)

    accs = ((u_acc, 0), (v_acc, LANES))

    def product(n, at, cut):
        return jnp.dot(
            arrived[n, at // LANES, cut, :], weights[n * LANES:(n + 1) * LANES, :],
            preferred_element_type=f32)

    every = slice(0, slots)

    def interp(g):
        n, span_of, lanes, halves = group_of(g)
        wait_bytes(arrived.at[span_of, lanes, others], ar_sem.at[g])
        for acc, at in accs:
            if at // LANES not in halves:
                continue
            if n == 0:
                acc[...] = product(n, at, every)
            else:
                acc[...] += product(n, at, every)

    for g in range(groups - 1):
        interp(g)
    wait_bytes(o_recv.at[pl.ds(0, blk - 1)], or_sem)
    per = LANES // cap
    group = 2 * LANES if slots % (2 * LANES) == 0 else LANES
    for g in range(blk // per):
        mark = o_recv[g * per]
        for j in range(1, per):
            mark = mark + o_recv[g * per + j]
        spot = iota((MAPH, LANES), 0) == mark.astype(jnp.int32) - 1
        spots[:, g * LANES:(g + 1) * LANES] = spot.astype(f32).astype(bf16)
    _, span_of, lanes, final = group_of(groups - 1)
    late = chunks - joined
    span_out = 2 * LANES

    def finish(turn):
        here = side if turn == 0 else 1 - side
        came_from = pl.ds(0, (blk // 2 - 1 + turn) * cap)
        wait_bytes(arrived.at[span_of, lanes, came_from], ar_sem.at[groups - 1 + here])
        for c in range(0, columns, span_out):
            to = slice(c, c + span_out)
            total = jnp.zeros((MAPH, span_out), f32)
            for g in range(slots // 2 // group):
                cut = pl.ds(pl.multiple_of(here * (slots // 2) + g * group, group), group)
                power = 0.0
                for acc, at in accs:
                    value = acc[cut, to]
                    if chunks > 1 and at // LANES in final:
                        came = jnp.concatenate(
                            [arrived[n, at // LANES, cut, :] for n in range(late, chunks)], axis=1)
                        value = value + jnp.dot(
                            came, weights[late * LANES:, to], preferred_element_type=f32)
                    power = power + value * value
                high = power.astype(bf16)
                mid = (power - high.astype(f32)).astype(bf16)
                for part in (high, mid):
                    total = total + jnp.dot(spots[:, cut], part, preferred_element_type=f32)
            if turn == 0:
                out_ref[:, to] = total
            else:
                out_ref[:, to] += total

    finish(0)
    finish(1)

    def sent(kind):
        for h in range(2):
            wait_bytes(half_of(0, h), g_send.at[kind, h])

    for kind in (0, 4, 5, 6):
        sent(kind)
    for kind, used in (
            (1, core == 1), (2, quad != 1), (3, quad != 3), (7, core == 0), (8, quad == 1), (9, quad == 2)):
        pl.when(used)(functools.partial(sent, kind))
    for s in range(parts):
        n, lanes, _ = part_of(s)
        wait_bytes(x_send.at[n, lanes], xs_sem.at[s])
    for g in range(groups):
        _, span_of, lanes, _ = group_of(g)
        wait_bytes(packed.at[span_of, lanes, others], as_sem.at[g])
    wait_bytes(o_send.at[pl.ds(0, blk - 1)], os_sem)


def body(phase_history, tile_curvature, interp_weights, strip_tiles, row_offsets, tile_owner):
    blk = lax.axis_size("blk")
    maps = lax.axis_size("map")
    pulses = phase_history.shape[2]
    freqs = phase_history.shape[3] // 2
    columns = interp_weights.shape[2]
    rows = strip_tiles.shape[2]
    cap = max(TILE, 2 * rows // blk)
    slots = blk * cap
    chunks = columns // LANES
    width = 2 * LANES
    stacked = STOPS // 2 * pulses
    f32, bf16 = jnp.float32, jnp.bfloat16
    hbm = pl.BlockSpec(memory_space=pltpu.HBM)
    vmem = pl.BlockSpec(memory_space=pltpu.VMEM)
    dma = pltpu.SemaphoreType.DMA
    in_hbm = functools.partial(pltpu.with_memory_space_constraint, memory_space=pltpu.HBM)
    out = pl.pallas_call(
        functools.partial(kernel, (blk, maps, pulses, freqs, columns, rows, cap)),
        out_shape=jax.ShapeDtypeStruct((MAPH, columns), f32),
        in_specs=[hbm, pl.BlockSpec(memory_space=pltpu.SMEM), hbm, hbm, hbm, hbm],
        out_specs=vmem,
        scratch_shapes=[
            pltpu.VMEM((columns, columns), bf16),
            pltpu.VMEM((1, rows), jnp.int32),
            pltpu.VMEM((1, rows), jnp.int32),
            pltpu.VMEM((1, blk), jnp.int32),
            dma((5,)),
            pltpu.VMEM((STOPS, 2, pulses, freqs), f32),
            pltpu.VMEM((STOPS, pulses, 2 * freqs), bf16),
            pltpu.VMEM((chunks, freqs, width), bf16),
            pltpu.VMEM((rows * maps, 2 * stacked), bf16),
            pltpu.VMEM((2, 2 * pulses, freqs), bf16),
            pltpu.VMEM((chunks, 2, 2 * stacked, width), bf16),
            pltpu.VMEM((columns, columns), bf16),
            pltpu.VMEM((chunks, 2, rows, LANES), bf16),
            pltpu.VMEM((chunks, 2, rows, LANES), bf16),
            pltpu.VMEM((chunks, 2, rows, LANES), f32),
            pltpu.VMEM((chunks, 2, slots, LANES), bf16),
            pltpu.VMEM((chunks, 2, slots, LANES), bf16),
            pltpu.VMEM((slots, rows), bf16),
            pltpu.VMEM((blk, 1, LANES), f32),
            pltpu.VMEM((blk, 1, LANES), f32),
            pltpu.VMEM((slots, columns), f32),
            pltpu.VMEM((slots, columns), f32),
            pltpu.VMEM((MAPH, slots), bf16),
            dma((10, 2)), dma((STOPS, 2)), dma((chunks + 1,)), dma((chunks + 1,)),
            dma((chunks + 1,)), dma((chunks + 2,)), dma, dma,
        ],
        compiler_params=pltpu.CompilerParams(
            collective_id=0, has_side_effects=True, vmem_limit_bytes=40 * 2**20),
    )(
        in_hbm(phase_history[0, 0]), tile_curvature, in_hbm(interp_weights[0]),
        in_hbm(strip_tiles[0, 0].reshape(1, rows)), in_hbm(row_offsets[0]),
        in_hbm(tile_owner.reshape(1, blk)),
    )
    return jnp.maximum(out, 0.0).reshape(1, 1, MAPH, columns)


def solution(mesh):
    in_specs = (
        P("blk", "map", None, None),
        P("blk"),
        P("blk", None, None),
        P("blk", "map", None, None),
        P("blk", "map", None),
        P(),
    )
    out_specs = P("blk", "map", None, None)
    return jax.shard_map(body, mesh=mesh, in_specs=in_specs, out_specs=out_specs, check_vma=False)
```

```python
import functools
import math

import jax
import jax.numpy as jnp
import numpy as np
from jax import lax
from jax.experimental import pallas as pl
from jax.experimental.pallas import tpu as pltpu
from jax.sharding import PartitionSpec as P

STOPS = 8
MAPH = 256
LANES = 128
TILE = 16


def fit_turns():
    z = 0.125 - 0.125 * np.cos(np.pi * (np.arange(400) + 0.5) / 400)
    t = np.sqrt(z)
    cheb = np.polynomial.chebyshev.Chebyshev
    cos_fit = cheb.fit(z, np.cos(2 * np.pi * t), 7, domain=[0, 0.25])
    sin_fit = cheb.fit(z, np.sin(2 * np.pi * t) / t, 6, domain=[0, 0.25])
    power = np.polynomial.Polynomial
    return (
        [float(np.float32(c)) for c in cos_fit.convert(kind=power).coef],
        [float(np.float32(c)) for c in sin_fit.convert(kind=power).coef],
    )


COS_COEF, SIN_COEF = fit_turns()


def cos_sin_turns(turns):
    t = turns - jnp.round(turns)
    z = t * t
    c = jnp.full_like(z, COS_COEF[-1])
    for coef in COS_COEF[-2::-1]:
        c = c * z + coef
    s = jnp.full_like(z, SIN_COEF[-1])
    for coef in SIN_COEF[-2::-1]:
        s = s * z + coef
    return c, s * t


def iota(shape, axis):
    return lax.broadcasted_iota(jnp.int32, shape, axis)


def kernel(
    sizes,
    block_hbm, curv_ref, weight_hbm, tiles_hbm, offs_hbm, owner_hbm,
    out_ref,
    weight_ref, tiles_ref, offs_ref, owner_ref, in_sem, trig, blocks, ranges, cross, phased, right, weights, x_send, x_recv, x_own, packed, arrived, slot_hot,
    o_send, o_recv, u_acc, v_acc, spots,
    g_send, g_recv, xs_sem, xr_sem, as_sem, ar_sem, os_sem, or_sem,
):
    blk, maps, pulses, freqs, columns, rows, cap = sizes
    f32, bf16 = jnp.float32, jnp.bfloat16
    me = lax.axis_index("blk")
    my_map = lax.axis_index("map")
    other_map = 1 - my_map
    core = lax.rem(me, 2)
    span = STOPS * maps * pulses
    stacked = STOPS // 2 * pulses
    chunks = columns // LANES
    width = 2 * LANES
    slots = blk * cap
    own_stop = STOPS // 2 - 1

    def device(index):
        return (lax.rem(index + 2 * blk, blk), my_map)

    mesh_id = pl.DeviceIdType.MESH

    barrier = pltpu.get_barrier_semaphore()

    def greet(i, _):
        pl.semaphore_signal(barrier, inc=1, device_id=device(me + i), device_id_type=mesh_id)
        return 0

    lax.fori_loop(1, blk, greet, 0)
    pl.semaphore_signal(barrier, inc=1, device_id=(me, other_map), device_id_type=mesh_id)

    def bring(source, target, sem):
        return pltpu.make_async_copy(source, target, in_sem.at[sem])

    inputs = [
        bring(block_hbm, blocks.at[own_stop], 0),
        bring(owner_hbm, owner_ref, 1),
        bring(tiles_hbm, tiles_ref, 2),
        bring(offs_hbm, offs_ref, 3),
        bring(weight_hbm, weight_ref, 4),
    ]
    for copy in inputs:
        copy.start()
    inputs[0].wait()
    pl.semaphore_wait(barrier, blk)

    partner = device(me + 1 - 2 * core)
    shift = 2 * core - 1
    quad = lax.rem(me, 4)
    half = pulses // 2
    last = 2 - core

    def half_of(stop, h):
        return blocks.at[stop, pl.ds(h * half, half)]

    def push(source, stop, h, target, kind):
        pltpu.make_async_remote_copy(
            src_ref=half_of(source, h), dst_ref=half_of(stop, h), send_sem=g_send.at[kind, h],
            recv_sem=g_recv.at[stop, h], device_id=target, device_id_type=mesh_id).start()

    def push_own(stop, target, kind):
        for h in range(2):
            push(own_stop, stop, h, target, kind)

    def arrived_half(stop, h):
        pltpu.make_async_copy(half_of(stop, h), half_of(stop, h), g_recv.at[stop, h]).wait()

    def arrived_block(stop):
        for h in range(2):
            arrived_half(stop, h)

    def pass_on(stop, to_stop, target, kind):
        for h in range(2):
            arrived_half(stop, h)
            push(stop, to_stop, h, target, kind)

    @pl.when(quad == 3)
    def _():
        push_own(0, device(me + 3), 1)

    push_own(7, device(me - 4), 0)

    @pl.when(quad == 1)
    def _():
        push_own(0, device(me + 3), 1)

    @pl.when(quad != 1)
    def _():
        push_own(5, device(me - 2), 2)

    @pl.when(quad != 3)
    def _():
        push_own(1, device(me + 2), 3)

    push_own(own_stop + shift, partner, 4)

    half_freqs = freqs // 2
    half_chunks = chunks // 2
    half_rows = rows // 2

    def fill_ranges(i, _):
        at = pl.ds(pl.multiple_of(i * TILE, TILE), TILE)
        below = pl.ds(pl.multiple_of(half_freqs + i * TILE, TILE), TILE)
        f = (i * TILE + iota((TILE, columns // 2), 0)).astype(f32)
        for odd in range(2):
            c = (2 * iota((TILE, columns // 2), 1) + odd).astype(f32)
            re, im = cos_sin_turns(f * c * (1.0 / freqs))
            re = (re * (1.0 / math.sqrt(freqs))).astype(bf16)
            im = (im * (1.0 / math.sqrt(freqs)))
            pos, neg = im.astype(bf16), (-im).astype(bf16)
            for n in range(half_chunks):
                cut = slice(n * LANES, (n + 1) * LANES)
                to = odd * half_chunks + n
                ranges[to, at, 0:LANES] = re[:, cut]
                ranges[to, at, LANES:width] = neg[:, cut]
                ranges[to, below, 0:LANES] = pos[:, cut]
                ranges[to, below, LANES:width] = re[:, cut]
        return 0

    lax.fori_loop(0, half_freqs // TILE, fill_ranges, 0)

    lane = iota((1, stacked), 1)
    q_lane = (lane + (lax.div(lane, pulses) * (maps - 1) + my_map) * pulses).astype(f32)

    def fill_cross(i, _):
        at = pl.ds(pl.multiple_of(i * TILE, TILE), TILE)
        g = i * TILE
        odd = lax.div(g, rows)
        own = lax.div(lax.rem(g, rows), half_rows)
        part = jnp.where(own == 1, my_map, other_map)
        base = part * rows + odd + 2 * lax.rem(g, half_rows)
        a = (base + 2 * iota((TILE, stacked), 0)).astype(f32)
        re, im = cos_sin_turns(a * q_lane * (1.0 / span))
        cross[at, 0:stacked] = (re * (1.0 / math.sqrt(span))).astype(bf16)
        cross[at, stacked:2 * stacked] = (im * (-1.0 / math.sqrt(span))).astype(bf16)
        return 0

    lax.fori_loop(0, rows * maps // TILE, fill_cross, 0)

    def fill_slots():
        tiles = tiles_ref[...]
        holders = iota((blk, rows), 0)
        named = (holders == tiles).astype(f32).astype(bf16)
        holds = (iota((blk, blk), 0) == owner_ref[...]).astype(f32).astype(bf16)
        hot = jnp.dot(holds, named, preferred_element_type=f32)
        dest = jnp.sum(holders.astype(f32) * hot, axis=0, keepdims=True).astype(jnp.int32)
        upto = (iota((rows, rows), 0) <= iota((rows, rows), 1)).astype(f32).astype(bf16)
        counts = jnp.dot(hot.astype(bf16), upto, preferred_element_type=f32)
        rank = jnp.sum(counts * hot, axis=0, keepdims=True).astype(jnp.int32) - 1
        slot = dest * cap + rank
        spot = iota((rows, rows), 1)
        spot = 2 * lax.rem(spot, half_rows) + lax.div(spot, half_rows)
        order = (iota((rows, rows), 0) == spot).astype(f32).astype(bf16)
        for i in range(slots // LANES):
            at = i * LANES + iota((LANES, rows), 0)
            hits = (at == slot).astype(f32).astype(bf16)
            slot_hot[i * LANES:(i + 1) * LANES, :] = jnp.dot(
                hits, order, preferred_element_type=f32).astype(bf16)
        place = lax.rem(me, LANES // cap) * cap + rank
        marks = jnp.where(iota((LANES, rows), 0) == place, (offs_ref[...] + 1).astype(f32), 0.0)
        table = lax.dot_general(
            hot.astype(bf16), marks.astype(bf16), (((1,), (1,)), ((), ())),
            preferred_element_type=f32)
        for d in range(blk):
            o_send[d] = table[d:d + 1, :]
        o_recv[me] = o_send[me]

        def send(i, _):
            to = lax.rem(me + i, blk)
            pltpu.make_async_remote_copy(
                src_ref=o_send.at[to], dst_ref=o_recv.at[me], send_sem=os_sem,
                recv_sem=or_sem, device_id=(to, my_map), device_id_type=mesh_id).start()
            return 0

        lax.fori_loop(1, blk, send, 0)

    for copy in inputs[1:]:
        copy.wait()
    fill_slots()

    def order_weights(i, _):
        at = pl.ds(pl.multiple_of(i * LANES, LANES), LANES)
        r = i * LANES + iota((LANES, columns), 0)
        r = 2 * lax.rem(r, columns // 2) + lax.div(r, columns // 2)
        order = (iota((LANES, columns), 1) == r).astype(f32).astype(bf16)
        weights[at, :] = jnp.dot(
            order, weight_ref[...], preferred_element_type=f32).astype(bf16)
        return 0

    lax.fori_loop(0, chunks, order_weights, 0)

    def fill_trig(i, _):
        at = pl.ds(pl.multiple_of(lax.rem(i, pulses // TILE) * TILE, TILE), TILE)
        k = lax.div(i, pulses // TILE)
        q = (k * maps + my_map) * pulses + lax.rem(i, pulses // TILE) * TILE + iota((TILE, 1), 0)
        s = q.astype(f32) * (1.0 / span) - 0.5
        r = iota((TILE, freqs), 1).astype(f32) * (1.0 / freqs) - 0.5
        angle = curv_ref[0] * (s * s) * (1.0 + r)
        c, si = cos_sin_turns(angle * (0.5 / math.pi))
        trig[k, 0, at, :] = c
        trig[k, 1, at, :] = si
        return 0

    lax.fori_loop(0, STOPS * pulses // TILE, fill_trig, 0)

    def turned(k, i):
        at = pl.ds(pl.multiple_of(i * TILE, TILE), TILE)
        c, si = trig[k, 0, at, :], trig[k, 1, at, :]
        re = blocks[k, at, 0:freqs].astype(f32)
        im = blocks[k, at, freqs:2 * freqs].astype(f32)
        return re * c - im * si, re * si + im * c

    def phase(j):
        def turn(i, _):
            first = turned(j, i)
            second = turned(j + STOPS // 2, i)
            for part in range(2):
                z_sum, z_diff = first[part] + second[part], first[part] - second[part]
                to = slice(part * half_freqs, (part + 1) * half_freqs)
                for odd_row, z in ((0, z_sum), (1, z_diff)):
                    at = pl.ds(pl.multiple_of(odd_row * pulses + i * TILE, TILE), TILE)
                    near, far = z[:, :half_freqs], z[:, half_freqs:]
                    phased[0, at, to] = (near + far).astype(bf16)
                    phased[1, at, to] = (near - far).astype(bf16)
            return 0

        lax.fori_loop(0, pulses // TILE, turn, 0, unroll=2)

    def spectrum(j, n):
        top = pl.ds(pl.multiple_of(j * pulses, pulses), pulses)
        low = pl.ds(pl.multiple_of(stacked + j * pulses, pulses), pulses)
        odd = lax.div(n, half_chunks)
        y = jnp.dot(phased[odd], ranges[n], preferred_element_type=f32)
        yr, yi = y[:, :LANES], y[:, LANES:]
        for odd_row in range(2):
            cut = slice(odd_row * pulses, (odd_row + 1) * pulses)
            real, imag = yr[cut].astype(bf16), yi[cut].astype(bf16)
            right[n, odd_row, top, 0:LANES] = real
            right[n, odd_row, top, LANES:width] = imag
            right[n, odd_row, low, 0:LANES] = (-yi[cut]).astype(bf16)
            right[n, odd_row, low, LANES:width] = real

    def near(stop):
        pass_on(stop, stop + shift, partner, jnp.where(stop == 5, 5, 6))

    near_stop = jnp.where(quad < 2, 5, 1)

    def step(i, _):
        j = jnp.where(i == 0, 3, jnp.where(i == 1, 2 * core, 1 - core))

        @pl.when(i == 0)
        def _():
            near(near_stop)

            @pl.when(quad == 1)
            def _():
                pass_on(7, 5, device(me + 2), 8)

            @pl.when(quad == 2)
            def _():
                pass_on(0, 1, device(me - 1), 9)

            @pl.when(core == 0)
            def _():
                pass_on(7, 6, partner, 7)

            @pl.when(quad == 3)
            def _():
                arrived_block(7)

        @pl.when(i == 1 + core)
        def _():
            near(6 - near_stop)

        @pl.when((j == 0) & (quad != 2))
        def _():
            arrived_block(0)

        @pl.when((j == 0) | (j == 2))
        def _():
            arrived_block(jnp.maximum(j, 0) + STOPS // 2)

        @pl.when(j == 2)
        def _():
            arrived_block(2)

        phase(j)
        for n in range(chunks):
            spectrum(j, n)
        return 0

    lax.fori_loop(0, STOPS // 2 - 1, step, 0)

    @pl.when(core == 0)
    def _():
        arrived_block(2)
        arrived_block(6)

    phase(last)
    first_parts = 2
    parts = chunks + first_parts - 1

    def part_of(s):
        if s < first_parts:
            return 0, pl.ds(s, 1), (s,)
        return s - first_parts + 1, pl.ds(0, 2), (0, 1)

    joined = 2 if chunks >= 4 else 1
    groups = parts - joined + 1

    def group_of(g):
        n, lanes, halves = part_of(g)
        return n, pl.ds(n, joined if g == groups - 1 else 1), lanes, halves

    def x_copy(s):
        n, lanes, _ = part_of(s)
        return pltpu.make_async_remote_copy(
            src_ref=x_send.at[n, lanes], dst_ref=x_recv.at[n, lanes], send_sem=xs_sem.at[s],
            recv_sem=xr_sem.at[s], device_id=(me, other_map), device_id_type=mesh_id)

    side = lax.div(me, blk // 2)
    own_slots = pl.ds(pl.multiple_of(me * cap, cap), cap)

    def early_copy(odd_row):
        at = pl.ds(odd_row * half_rows, half_rows)
        sem = parts * odd_row
        return pltpu.make_async_remote_copy(
            src_ref=x_send.at[0, pl.ds(0, 1), at], dst_ref=x_recv.at[0, pl.ds(0, 1), at],
            send_sem=xs_sem.at[sem], recv_sem=xr_sem.at[sem], device_id=(me, other_map),
            device_id_type=mesh_id)

    def produce(n):
        spectrum(last, n)
        for odd_row in range(2):
            table = cross[odd_row * rows:(odd_row + 1) * rows, :]
            y = jnp.dot(table, right[n, odd_row], preferred_element_type=f32)
            to = slice(odd_row * half_rows, (odd_row + 1) * half_rows)
            for p in range(2):
                cut = slice(p * LANES, (p + 1) * LANES)
                x_send[n, p, to, :] = y[:half_rows, cut].astype(bf16)
                x_own[n, p, to, :] = y[half_rows:, cut]
            if n == 0:
                early_copy(odd_row).start()
        for s in range(parts):
            if s > 0 and part_of(s)[0] == n:
                x_copy(s).start()

    def route(s):
        n, lanes, halves = part_of(s)
        if s == 0:
            early_copy(0).wait_recv()
            early_copy(1).wait_recv()
        else:
            x_copy(s).wait_recv()
        image = jnp.concatenate([
            (x_own[n, p] + x_recv[n, p].astype(f32)).astype(bf16) for p in halves], axis=1)
        slotted = jnp.dot(slot_hot[...], image, preferred_element_type=f32).astype(bf16)
        for at, p in enumerate(halves):
            packed[n, p] = slotted[:, at * LANES:(at + 1) * LANES]

        for p in halves:
            arrived[n, p, own_slots, :] = packed[n, p, own_slots, :]
        if groups - 1 <= s < parts - 1:
            return
        g = min(s, groups - 1)
        _, span_of, lanes, _ = group_of(g)

        def send(i, _):
            to = jnp.where(i - 1 < me, i - 1, i) if g == groups - 1 else lax.rem(me + i, blk)
            pltpu.make_async_remote_copy(
                src_ref=packed.at[span_of, lanes, pl.ds(pl.multiple_of(to * cap, cap), cap)],
                dst_ref=arrived.at[span_of, lanes, own_slots], send_sem=as_sem.at[g],
                recv_sem=ar_sem.at[g + (side if g == groups - 1 else 0)], device_id=(to, my_map),
                device_id_type=mesh_id).start()
            return 0

        lax.fori_loop(1, blk, send, 0)

    produce(0)
    for s in range(parts):
        n = part_of(s)[0]
        if (s == 0 or part_of(s - 1)[0] != n) and n + 1 < chunks:
            produce(n + 1)
        route(s)

    def wait_bytes(ref, sem):
        pltpu.make_async_copy(ref, ref, sem).wait()

    others = pl.ds(0, (blk - 1) * cap)

    accs = ((u_acc, 0), (v_acc, LANES))

    def product(n, at, cut):
        return jnp.dot(
            arrived[n, at // LANES, cut, :], weights[n * LANES:(n + 1) * LANES, :],
            preferred_element_type=f32)

    every = slice(0, slots)

    def interp(g):
        n, span_of, lanes, halves = group_of(g)
        wait_bytes(arrived.at[span_of, lanes, others], ar_sem.at[g])
        for acc, at in accs:
            if at // LANES not in halves:
                continue
            if n == 0:
                acc[...] = product(n, at, every)
            else:
                acc[...] += product(n, at, every)

    for g in range(groups - 1):
        interp(g)
    wait_bytes(o_recv.at[pl.ds(0, blk - 1)], or_sem)
    per = LANES // cap
    group = 2 * LANES if slots % (2 * LANES) == 0 else LANES
    for g in range(blk // per):
        mark = o_recv[g * per]
        for j in range(1, per):
            mark = mark + o_recv[g * per + j]
        spot = iota((MAPH, LANES), 0) == mark.astype(jnp.int32) - 1
        spots[:, g * LANES:(g + 1) * LANES] = spot.astype(f32).astype(bf16)
    _, span_of, lanes, final = group_of(groups - 1)
    late = chunks - joined
    span_out = 2 * LANES

    def finish(turn):
        here = side if turn == 0 else 1 - side
        came_from = pl.ds(0, (blk // 2 - 1 + turn) * cap)
        wait_bytes(arrived.at[span_of, lanes, came_from], ar_sem.at[groups - 1 + here])
        for c in range(0, columns, span_out):
            to = slice(c, c + span_out)
            total = jnp.zeros((MAPH, span_out), f32)
            for g in range(slots // 2 // group):
                cut = pl.ds(pl.multiple_of(here * (slots // 2) + g * group, group), group)
                power = 0.0
                for acc, at in accs:
                    value = acc[cut, to]
                    if chunks > 1 and at // LANES in final:
                        came = jnp.concatenate(
                            [arrived[n, at // LANES, cut, :] for n in range(late, chunks)], axis=1)
                        value = value + jnp.dot(
                            came, weights[late * LANES:, to], preferred_element_type=f32)
                    power = power + value * value
                high = power.astype(bf16)
                mid = (power - high.astype(f32)).astype(bf16)
                for part in (high, mid):
                    total = total + jnp.dot(spots[:, cut], part, preferred_element_type=f32)
            if turn == 0:
                out_ref[:, to] = total
            else:
                out_ref[:, to] += total

    finish(0)
    finish(1)

    def sent(kind):
        for h in range(2):
            wait_bytes(half_of(0, h), g_send.at[kind, h])

    for kind in (0, 4, 5, 6):
        sent(kind)
    for kind, used in (
            (1, core == 1), (2, quad != 1), (3, quad != 3), (7, core == 0), (8, quad == 1), (9, quad == 2)):
        pl.when(used)(functools.partial(sent, kind))
    for s in range(parts):
        n, lanes, _ = part_of(s)
        if s == 0:
            early_copy(0).wait_send()
            early_copy(1).wait_send()
        else:
            wait_bytes(x_send.at[n, lanes], xs_sem.at[s])
    for g in range(groups):
        _, span_of, lanes, _ = group_of(g)
        wait_bytes(packed.at[span_of, lanes, others], as_sem.at[g])
    wait_bytes(o_send.at[pl.ds(0, blk - 1)], os_sem)


def body(phase_history, tile_curvature, interp_weights, strip_tiles, row_offsets, tile_owner):
    blk = lax.axis_size("blk")
    maps = lax.axis_size("map")
    pulses = phase_history.shape[2]
    freqs = phase_history.shape[3] // 2
    columns = interp_weights.shape[2]
    rows = strip_tiles.shape[2]
    cap = max(TILE, 2 * rows // blk)
    slots = blk * cap
    chunks = columns // LANES
    width = 2 * LANES
    stacked = STOPS // 2 * pulses
    f32, bf16 = jnp.float32, jnp.bfloat16
    hbm = pl.BlockSpec(memory_space=pltpu.HBM)
    vmem = pl.BlockSpec(memory_space=pltpu.VMEM)
    dma = pltpu.SemaphoreType.DMA
    in_hbm = functools.partial(pltpu.with_memory_space_constraint, memory_space=pltpu.HBM)
    out = pl.pallas_call(
        functools.partial(kernel, (blk, maps, pulses, freqs, columns, rows, cap)),
        out_shape=jax.ShapeDtypeStruct((MAPH, columns), f32),
        in_specs=[hbm, pl.BlockSpec(memory_space=pltpu.SMEM), hbm, hbm, hbm, hbm],
        out_specs=vmem,
        scratch_shapes=[
            pltpu.VMEM((columns, columns), bf16),
            pltpu.VMEM((1, rows), jnp.int32),
            pltpu.VMEM((1, rows), jnp.int32),
            pltpu.VMEM((1, blk), jnp.int32),
            dma((5,)),
            pltpu.VMEM((STOPS, 2, pulses, freqs), f32),
            pltpu.VMEM((STOPS, pulses, 2 * freqs), bf16),
            pltpu.VMEM((chunks, freqs, width), bf16),
            pltpu.VMEM((rows * maps, 2 * stacked), bf16),
            pltpu.VMEM((2, 2 * pulses, freqs), bf16),
            pltpu.VMEM((chunks, 2, 2 * stacked, width), bf16),
            pltpu.VMEM((columns, columns), bf16),
            pltpu.VMEM((chunks, 2, rows, LANES), bf16),
            pltpu.VMEM((chunks, 2, rows, LANES), bf16),
            pltpu.VMEM((chunks, 2, rows, LANES), f32),
            pltpu.VMEM((chunks, 2, slots, LANES), bf16),
            pltpu.VMEM((chunks, 2, slots, LANES), bf16),
            pltpu.VMEM((slots, rows), bf16),
            pltpu.VMEM((blk, 1, LANES), f32),
            pltpu.VMEM((blk, 1, LANES), f32),
            pltpu.VMEM((slots, columns), f32),
            pltpu.VMEM((slots, columns), f32),
            pltpu.VMEM((MAPH, slots), bf16),
            dma((10, 2)), dma((STOPS, 2)), dma((chunks + 2,)), dma((chunks + 2,)),
            dma((chunks + 1,)), dma((chunks + 2,)), dma, dma,
        ],
        compiler_params=pltpu.CompilerParams(
            collective_id=0, has_side_effects=True, vmem_limit_bytes=40 * 2**20),
    )(
        in_hbm(phase_history[0, 0]), tile_curvature, in_hbm(interp_weights[0]),
        in_hbm(strip_tiles[0, 0].reshape(1, rows)), in_hbm(row_offsets[0]),
        in_hbm(tile_owner.reshape(1, blk)),
    )
    return jnp.maximum(out, 0.0).reshape(1, 1, MAPH, columns)


def solution(mesh):
    in_specs = (
        P("blk", "map", None, None),
        P("blk"),
        P("blk", None, None),
        P("blk", "map", None, None),
        P("blk", "map", None),
        P(),
    )
    out_specs = P("blk", "map", None, None)
    return jax.shard_map(body, mesh=mesh, in_specs=in_specs, out_specs=out_specs, check_vma=False)
```

```python
import functools
import math

import jax
import jax.numpy as jnp
import numpy as np
from jax import lax
from jax.experimental import pallas as pl
from jax.experimental.pallas import tpu as pltpu
from jax.sharding import PartitionSpec as P

STOPS = 8
MAPH = 256
LANES = 128
TILE = 16


def fit_turns():
    z = 0.125 - 0.125 * np.cos(np.pi * (np.arange(400) + 0.5) / 400)
    t = np.sqrt(z)
    cheb = np.polynomial.chebyshev.Chebyshev
    cos_fit = cheb.fit(z, np.cos(2 * np.pi * t), 7, domain=[0, 0.25])
    sin_fit = cheb.fit(z, np.sin(2 * np.pi * t) / t, 6, domain=[0, 0.25])
    power = np.polynomial.Polynomial
    return (
        [float(np.float32(c)) for c in cos_fit.convert(kind=power).coef],
        [float(np.float32(c)) for c in sin_fit.convert(kind=power).coef],
    )


COS_COEF, SIN_COEF = fit_turns()


def cos_sin_turns(turns):
    t = turns - jnp.round(turns)
    z = t * t
    c = jnp.full_like(z, COS_COEF[-1])
    for coef in COS_COEF[-2::-1]:
        c = c * z + coef
    s = jnp.full_like(z, SIN_COEF[-1])
    for coef in SIN_COEF[-2::-1]:
        s = s * z + coef
    return c, s * t


def iota(shape, axis):
    return lax.broadcasted_iota(jnp.int32, shape, axis)


def kernel(
    sizes,
    block_hbm, curv_ref, weight_hbm, tiles_hbm, offs_hbm, owner_hbm,
    out_ref,
    weight_ref, tiles_ref, offs_ref, owner_ref, in_sem, trig, blocks, ranges, cross, phased, right, weights, x_send, x_recv, x_own, packed, arrived, slot_hot,
    o_send, o_recv, u_acc, v_acc, spots,
    g_send, g_recv, xs_sem, xr_sem, as_sem, ar_sem, os_sem, or_sem,
):
    blk, maps, pulses, freqs, columns, rows, cap = sizes
    f32, bf16 = jnp.float32, jnp.bfloat16
    me = lax.axis_index("blk")
    my_map = lax.axis_index("map")
    other_map = 1 - my_map
    core = lax.rem(me, 2)
    span = STOPS * maps * pulses
    stacked = STOPS // 2 * pulses
    chunks = columns // LANES
    width = 2 * LANES
    slots = blk * cap
    own_stop = STOPS // 2 - 1

    def device(index):
        return (lax.rem(index + 2 * blk, blk), my_map)

    mesh_id = pl.DeviceIdType.MESH

    barrier = pltpu.get_barrier_semaphore()

    def greet(i, _):
        pl.semaphore_signal(barrier, inc=1, device_id=device(me + i), device_id_type=mesh_id)
        return 0

    lax.fori_loop(1, blk, greet, 0)
    pl.semaphore_signal(barrier, inc=1, device_id=(me, other_map), device_id_type=mesh_id)

    def bring(source, target, sem):
        return pltpu.make_async_copy(source, target, in_sem.at[sem])

    inputs = [
        bring(block_hbm, blocks.at[own_stop], 0),
        bring(owner_hbm, owner_ref, 1),
        bring(tiles_hbm, tiles_ref, 2),
        bring(offs_hbm, offs_ref, 3),
        bring(weight_hbm, weight_ref, 4),
    ]
    for copy in inputs:
        copy.start()
    inputs[0].wait()
    pl.semaphore_wait(barrier, blk)

    partner = device(me + 1 - 2 * core)
    shift = 2 * core - 1
    quad = lax.rem(me, 4)
    half = pulses // 2
    last = 2 - core

    def half_of(stop, h):
        return blocks.at[stop, pl.ds(h * half, half)]

    def push(source, stop, h, target, kind):
        pltpu.make_async_remote_copy(
            src_ref=half_of(source, h), dst_ref=half_of(stop, h), send_sem=g_send.at[kind, h],
            recv_sem=g_recv.at[stop, h], device_id=target, device_id_type=mesh_id).start()

    def push_own(stop, target, kind):
        for h in range(2):
            push(own_stop, stop, h, target, kind)

    def arrived_half(stop, h):
        pltpu.make_async_copy(half_of(stop, h), half_of(stop, h), g_recv.at[stop, h]).wait()

    def arrived_block(stop):
        for h in range(2):
            arrived_half(stop, h)

    def pass_on(stop, to_stop, target, kind):
        for h in range(2):
            arrived_half(stop, h)
            push(stop, to_stop, h, target, kind)

    @pl.when(quad == 3)
    def _():
        push_own(0, device(me + 3), 1)

    push_own(7, device(me - 4), 0)

    @pl.when(quad == 1)
    def _():
        push_own(0, device(me + 3), 1)

    @pl.when(quad != 1)
    def _():
        push_own(5, device(me - 2), 2)

    @pl.when(quad != 3)
    def _():
        push_own(1, device(me + 2), 3)

    push_own(own_stop + shift, partner, 4)

    half_freqs = freqs // 2
    half_chunks = chunks // 2
    half_rows = rows // 2

    def fill_ranges(i, _):
        at = pl.ds(pl.multiple_of(i * TILE, TILE), TILE)
        below = pl.ds(pl.multiple_of(half_freqs + i * TILE, TILE), TILE)
        f = (i * TILE + iota((TILE, columns // 2), 0)).astype(f32)
        for odd in range(2):
            c = (2 * iota((TILE, columns // 2), 1) + odd).astype(f32)
            re, im = cos_sin_turns(f * c * (1.0 / freqs))
            re = (re * (1.0 / math.sqrt(freqs))).astype(bf16)
            im = (im * (1.0 / math.sqrt(freqs)))
            pos, neg = im.astype(bf16), (-im).astype(bf16)
            for n in range(half_chunks):
                cut = slice(n * LANES, (n + 1) * LANES)
                to = odd * half_chunks + n
                ranges[to, at, 0:LANES] = re[:, cut]
                ranges[to, at, LANES:width] = neg[:, cut]
                ranges[to, below, 0:LANES] = pos[:, cut]
                ranges[to, below, LANES:width] = re[:, cut]
        return 0

    lax.fori_loop(0, half_freqs // TILE, fill_ranges, 0)

    lane = iota((1, stacked), 1)
    q_lane = (lane + (lax.div(lane, pulses) * (maps - 1) + my_map) * pulses).astype(f32)

    def fill_cross(i, _):
        at = pl.ds(pl.multiple_of(i * TILE, TILE), TILE)
        g = i * TILE
        odd = lax.div(g, rows)
        own = lax.div(lax.rem(g, rows), half_rows)
        part = jnp.where(own == 1, my_map, other_map)
        base = part * rows + odd + 2 * lax.rem(g, half_rows)
        a = (base + 2 * iota((TILE, stacked), 0)).astype(f32)
        re, im = cos_sin_turns(a * q_lane * (1.0 / span))
        cross[at, 0:stacked] = (re * (1.0 / math.sqrt(span))).astype(bf16)
        cross[at, stacked:2 * stacked] = (im * (-1.0 / math.sqrt(span))).astype(bf16)
        return 0

    lax.fori_loop(0, rows * maps // TILE, fill_cross, 0)

    def fill_slots():
        tiles = tiles_ref[...]
        holders = iota((blk, rows), 0)
        named = (holders == tiles).astype(f32).astype(bf16)
        holds = (iota((blk, blk), 0) == owner_ref[...]).astype(f32).astype(bf16)
        hot = jnp.dot(holds, named, preferred_element_type=f32)
        dest = jnp.sum(holders.astype(f32) * hot, axis=0, keepdims=True).astype(jnp.int32)
        upto = (iota((rows, rows), 0) <= iota((rows, rows), 1)).astype(f32).astype(bf16)
        counts = jnp.dot(hot.astype(bf16), upto, preferred_element_type=f32)
        rank = jnp.sum(counts * hot, axis=0, keepdims=True).astype(jnp.int32) - 1
        slot = dest * cap + rank
        spot = iota((rows, rows), 1)
        spot = 2 * lax.rem(spot, half_rows) + lax.div(spot, half_rows)
        order = (iota((rows, rows), 0) == spot).astype(f32).astype(bf16)
        for i in range(slots // LANES):
            at = i * LANES + iota((LANES, rows), 0)
            hits = (at == slot).astype(f32).astype(bf16)
            slot_hot[i * LANES:(i + 1) * LANES, :] = jnp.dot(
                hits, order, preferred_element_type=f32).astype(bf16)
        place = lax.rem(me, LANES // cap) * cap + rank
        marks = jnp.where(iota((LANES, rows), 0) == place, (offs_ref[...] + 1).astype(f32), 0.0)
        table = lax.dot_general(
            hot.astype(bf16), marks.astype(bf16), (((1,), (1,)), ((), ())),
            preferred_element_type=f32)
        for d in range(blk):
            o_send[d] = table[d:d + 1, :]
        o_recv[me] = o_send[me]

        def send(i, _):
            to = lax.rem(me + i, blk)
            pltpu.make_async_remote_copy(
                src_ref=o_send.at[to], dst_ref=o_recv.at[me], send_sem=os_sem,
                recv_sem=or_sem, device_id=(to, my_map), device_id_type=mesh_id).start()
            return 0

        lax.fori_loop(1, blk, send, 0)

    for copy in inputs[1:]:
        copy.wait()
    fill_slots()

    def order_weights(i, _):
        at = pl.ds(pl.multiple_of(i * LANES, LANES), LANES)
        r = i * LANES + iota((LANES, columns), 0)
        r = 2 * lax.rem(r, columns // 2) + lax.div(r, columns // 2)
        order = (iota((LANES, columns), 1) == r).astype(f32).astype(bf16)
        weights[at, :] = jnp.dot(
            order, weight_ref[...], preferred_element_type=f32).astype(bf16)
        return 0

    lax.fori_loop(0, chunks, order_weights, 0)

    def fill_trig(i, _):
        at = pl.ds(pl.multiple_of(lax.rem(i, pulses // TILE) * TILE, TILE), TILE)
        k = lax.div(i, pulses // TILE)
        q = (k * maps + my_map) * pulses + lax.rem(i, pulses // TILE) * TILE + iota((TILE, 1), 0)
        s = q.astype(f32) * (1.0 / span) - 0.5
        r = iota((TILE, freqs), 1).astype(f32) * (1.0 / freqs) - 0.5
        angle = curv_ref[0] * (s * s) * (1.0 + r)
        c, si = cos_sin_turns(angle * (0.5 / math.pi))
        trig[k, 0, at, :] = c
        trig[k, 1, at, :] = si
        return 0

    lax.fori_loop(0, STOPS * pulses // TILE, fill_trig, 0)

    def turned(k, i):
        at = pl.ds(pl.multiple_of(i * TILE, TILE), TILE)
        c, si = trig[k, 0, at, :], trig[k, 1, at, :]
        re = blocks[k, at, 0:freqs].astype(f32)
        im = blocks[k, at, freqs:2 * freqs].astype(f32)
        return re * c - im * si, re * si + im * c

    def phase(j):
        def turn(i, _):
            first = turned(j, i)
            second = turned(j + STOPS // 2, i)
            for part in range(2):
                z_sum, z_diff = first[part] + second[part], first[part] - second[part]
                to = slice(part * half_freqs, (part + 1) * half_freqs)
                for odd_row, z in ((0, z_sum), (1, z_diff)):
                    at = pl.ds(pl.multiple_of(odd_row * pulses + i * TILE, TILE), TILE)
                    near, far = z[:, :half_freqs], z[:, half_freqs:]
                    phased[0, at, to] = (near + far).astype(bf16)
                    phased[1, at, to] = (near - far).astype(bf16)
            return 0

        lax.fori_loop(0, pulses // TILE, turn, 0, unroll=2)

    def spectrum(j, n):
        top = pl.ds(pl.multiple_of(j * pulses, pulses), pulses)
        low = pl.ds(pl.multiple_of(stacked + j * pulses, pulses), pulses)
        odd = lax.div(n, half_chunks)
        y = jnp.dot(phased[odd], ranges[n], preferred_element_type=f32)
        yr, yi = y[:, :LANES], y[:, LANES:]
        for odd_row in range(2):
            cut = slice(odd_row * pulses, (odd_row + 1) * pulses)
            real, imag = yr[cut].astype(bf16), yi[cut].astype(bf16)
            right[n, odd_row, top, 0:LANES] = real
            right[n, odd_row, top, LANES:width] = imag
            right[n, odd_row, low, 0:LANES] = (-yi[cut]).astype(bf16)
            right[n, odd_row, low, LANES:width] = real

    def near(stop):
        pass_on(stop, stop + shift, partner, jnp.where(stop == 5, 5, 6))

    near_stop = jnp.where(quad < 2, 5, 1)

    def step(i, _):
        j = jnp.where(i == 0, 3, jnp.where(i == 1, 2 * core, 1 - core))

        @pl.when(i == 0)
        def _():
            near(near_stop)

            @pl.when(quad == 1)
            def _():
                pass_on(7, 5, device(me + 2), 8)

            @pl.when(quad == 2)
            def _():
                pass_on(0, 1, device(me - 1), 9)

            @pl.when(core == 0)
            def _():
                pass_on(7, 6, partner, 7)

            @pl.when(quad == 3)
            def _():
                arrived_block(7)

        @pl.when(i == 1 + core)
        def _():
            near(6 - near_stop)

        @pl.when((j == 0) & (quad != 2))
        def _():
            arrived_block(0)

        @pl.when((j == 0) | (j == 2))
        def _():
            arrived_block(jnp.maximum(j, 0) + STOPS // 2)

        @pl.when(j == 2)
        def _():
            arrived_block(2)

        phase(j)
        for n in range(chunks):
            spectrum(j, n)
        return 0

    lax.fori_loop(0, STOPS // 2 - 1, step, 0)

    @pl.when(core == 0)
    def _():
        arrived_block(2)
        arrived_block(6)

    phase(last)
    first_parts = 2
    parts = chunks + first_parts - 1

    def part_of(s):
        if s < first_parts:
            return 0, pl.ds(s, 1), (s,)
        return s - first_parts + 1, pl.ds(0, 2), (0, 1)

    joined = 2 if chunks >= 4 else 1
    groups = parts - joined + 1

    def group_of(g):
        n, lanes, halves = part_of(g)
        return n, pl.ds(n, joined if g == groups - 1 else 1), lanes, halves

    def x_copy(s):
        n, lanes, _ = part_of(s)
        return pltpu.make_async_remote_copy(
            src_ref=x_send.at[n, lanes], dst_ref=x_recv.at[n, lanes], send_sem=xs_sem.at[s],
            recv_sem=xr_sem.at[s], device_id=(me, other_map), device_id_type=mesh_id)

    side = lax.div(me, blk // 2)
    own_slots = pl.ds(pl.multiple_of(me * cap, cap), cap)

    def produce(n):
        spectrum(last, n)
        for odd_row in range(2):
            table = cross[odd_row * rows:(odd_row + 1) * rows, :]
            y = jnp.dot(table, right[n, odd_row], preferred_element_type=f32)
            to = slice(odd_row * half_rows, (odd_row + 1) * half_rows)
            for p in range(2):
                cut = slice(p * LANES, (p + 1) * LANES)
                x_send[n, p, to, :] = y[:half_rows, cut].astype(bf16)
                x_own[n, p, to, :] = y[half_rows:, cut]
        for s in range(parts):
            if part_of(s)[0] == n:
                x_copy(s).start()

    def route(s):
        n, lanes, halves = part_of(s)
        x_copy(s).wait_recv()
        image = jnp.concatenate([
            (x_own[n, p] + x_recv[n, p].astype(f32)).astype(bf16) for p in halves], axis=1)
        slotted = jnp.dot(slot_hot[...], image, preferred_element_type=f32).astype(bf16)
        for at, p in enumerate(halves):
            packed[n, p] = slotted[:, at * LANES:(at + 1) * LANES]

        for p in halves:
            arrived[n, p, own_slots, :] = packed[n, p, own_slots, :]
        if groups - 1 <= s < parts - 1:
            return
        g = min(s, groups - 1)
        _, span_of, lanes, _ = group_of(g)

        def send(i, _):
            to = jnp.where(i - 1 < me, i - 1, i) if g == groups - 1 else lax.rem(me + i, blk)
            pltpu.make_async_remote_copy(
                src_ref=packed.at[span_of, lanes, pl.ds(pl.multiple_of(to * cap, cap), cap)],
                dst_ref=arrived.at[span_of, lanes, own_slots], send_sem=as_sem.at[g],
                recv_sem=ar_sem.at[g + (side if g == groups - 1 else 0)], device_id=(to, my_map),
                device_id_type=mesh_id).start()
            return 0

        lax.fori_loop(1, blk, send, 0, unroll=3)

    produce(0)
    for s in range(parts):
        n = part_of(s)[0]
        if (s == 0 or part_of(s - 1)[0] != n) and n + 1 < chunks:
            produce(n + 1)
        route(s)

    def wait_bytes(ref, sem):
        pltpu.make_async_copy(ref, ref, sem).wait()

    others = pl.ds(0, (blk - 1) * cap)

    accs = ((u_acc, 0), (v_acc, LANES))

    def product(n, at, cut):
        return jnp.dot(
            arrived[n, at // LANES, cut, :], weights[n * LANES:(n + 1) * LANES, :],
            preferred_element_type=f32)

    every = slice(0, slots)

    def interp(g):
        n, span_of, lanes, halves = group_of(g)
        wait_bytes(arrived.at[span_of, lanes, others], ar_sem.at[g])
        for acc, at in accs:
            if at // LANES not in halves:
                continue
            if n == 0:
                acc[...] = product(n, at, every)
            else:
                acc[...] += product(n, at, every)

    for g in range(groups - 1):
        interp(g)
    wait_bytes(o_recv.at[pl.ds(0, blk - 1)], or_sem)
    per = LANES // cap
    group = 2 * LANES if slots % (2 * LANES) == 0 else LANES
    for g in range(blk // per):
        mark = o_recv[g * per]
        for j in range(1, per):
            mark = mark + o_recv[g * per + j]
        spot = iota((MAPH, LANES), 0) == mark.astype(jnp.int32) - 1
        spots[:, g * LANES:(g + 1) * LANES] = spot.astype(f32).astype(bf16)
    _, span_of, lanes, final = group_of(groups - 1)
    late = chunks - joined
    span_out = 2 * LANES

    def finish(turn):
        here = side if turn == 0 else 1 - side
        came_from = pl.ds(0, (blk // 2 - 1 + turn) * cap)
        wait_bytes(arrived.at[span_of, lanes, came_from], ar_sem.at[groups - 1 + here])
        for c in range(0, columns, span_out):
            to = slice(c, c + span_out)
            total = jnp.zeros((MAPH, span_out), f32)
            for g in range(slots // 2 // group):
                cut = pl.ds(pl.multiple_of(here * (slots // 2) + g * group, group), group)
                power = 0.0
                for acc, at in accs:
                    value = acc[cut, to]
                    if chunks > 1 and at // LANES in final:
                        came = jnp.concatenate(
                            [arrived[n, at // LANES, cut, :] for n in range(late, chunks)], axis=1)
                        value = value + jnp.dot(
                            came, weights[late * LANES:, to], preferred_element_type=f32)
                    power = power + value * value
                high = power.astype(bf16)
                mid = (power - high.astype(f32)).astype(bf16)
                for part in (high, mid):
                    total = total + jnp.dot(spots[:, cut], part, preferred_element_type=f32)
            if turn == 0:
                out_ref[:, to] = total
            else:
                out_ref[:, to] += total

    finish(0)
    finish(1)

    def sent(kind):
        for h in range(2):
            wait_bytes(half_of(0, h), g_send.at[kind, h])

    for kind in (0, 4, 5, 6):
        sent(kind)
    for kind, used in (
            (1, core == 1), (2, quad != 1), (3, quad != 3), (7, core == 0), (8, quad == 1), (9, quad == 2)):
        pl.when(used)(functools.partial(sent, kind))
    for s in range(parts):
        n, lanes, _ = part_of(s)
        wait_bytes(x_send.at[n, lanes], xs_sem.at[s])
    for g in range(groups):
        _, span_of, lanes, _ = group_of(g)
        wait_bytes(packed.at[span_of, lanes, others], as_sem.at[g])
    wait_bytes(o_send.at[pl.ds(0, blk - 1)], os_sem)


def body(phase_history, tile_curvature, interp_weights, strip_tiles, row_offsets, tile_owner):
    blk = lax.axis_size("blk")
    maps = lax.axis_size("map")
    pulses = phase_history.shape[2]
    freqs = phase_history.shape[3] // 2
    columns = interp_weights.shape[2]
    rows = strip_tiles.shape[2]
    cap = max(TILE, 2 * rows // blk)
    slots = blk * cap
    chunks = columns // LANES
    width = 2 * LANES
    stacked = STOPS // 2 * pulses
    f32, bf16 = jnp.float32, jnp.bfloat16
    hbm = pl.BlockSpec(memory_space=pltpu.HBM)
    vmem = pl.BlockSpec(memory_space=pltpu.VMEM)
    dma = pltpu.SemaphoreType.DMA
    in_hbm = functools.partial(pltpu.with_memory_space_constraint, memory_space=pltpu.HBM)
    out = pl.pallas_call(
        functools.partial(kernel, (blk, maps, pulses, freqs, columns, rows, cap)),
        out_shape=jax.ShapeDtypeStruct((MAPH, columns), f32),
        in_specs=[hbm, pl.BlockSpec(memory_space=pltpu.SMEM), hbm, hbm, hbm, hbm],
        out_specs=vmem,
        scratch_shapes=[
            pltpu.VMEM((columns, columns), bf16),
            pltpu.VMEM((1, rows), jnp.int32),
            pltpu.VMEM((1, rows), jnp.int32),
            pltpu.VMEM((1, blk), jnp.int32),
            dma((5,)),
            pltpu.VMEM((STOPS, 2, pulses, freqs), f32),
            pltpu.VMEM((STOPS, pulses, 2 * freqs), bf16),
            pltpu.VMEM((chunks, freqs, width), bf16),
            pltpu.VMEM((rows * maps, 2 * stacked), bf16),
            pltpu.VMEM((2, 2 * pulses, freqs), bf16),
            pltpu.VMEM((chunks, 2, 2 * stacked, width), bf16),
            pltpu.VMEM((columns, columns), bf16),
            pltpu.VMEM((chunks, 2, rows, LANES), bf16),
            pltpu.VMEM((chunks, 2, rows, LANES), bf16),
            pltpu.VMEM((chunks, 2, rows, LANES), f32),
            pltpu.VMEM((chunks, 2, slots, LANES), bf16),
            pltpu.VMEM((chunks, 2, slots, LANES), bf16),
            pltpu.VMEM((slots, rows), bf16),
            pltpu.VMEM((blk, 1, LANES), f32),
            pltpu.VMEM((blk, 1, LANES), f32),
            pltpu.VMEM((slots, columns), f32),
            pltpu.VMEM((slots, columns), f32),
            pltpu.VMEM((MAPH, slots), bf16),
            dma((10, 2)), dma((STOPS, 2)), dma((chunks + 1,)), dma((chunks + 1,)),
            dma((chunks + 1,)), dma((chunks + 2,)), dma, dma,
        ],
        compiler_params=pltpu.CompilerParams(
            collective_id=0, has_side_effects=True, vmem_limit_bytes=40 * 2**20),
    )(
        in_hbm(phase_history[0, 0]), tile_curvature, in_hbm(interp_weights[0]),
        in_hbm(strip_tiles[0, 0].reshape(1, rows)), in_hbm(row_offsets[0]),
        in_hbm(tile_owner.reshape(1, blk)),
    )
    return jnp.maximum(out, 0.0).reshape(1, 1, MAPH, columns)


def solution(mesh):
    in_specs = (
        P("blk", "map", None, None),
        P("blk"),
        P("blk", None, None),
        P("blk", "map", None, None),
        P("blk", "map", None),
        P(),
    )
    out_specs = P("blk", "map", None, None)
    return jax.shard_map(body, mesh=mesh, in_specs=in_specs, out_specs=out_specs, check_vma=False)
```
